32 devices in a mesh: clus: 8 (over y, x, core), probe: 4 (over z).
Axes of the slice: x: 2, y: 2, z: 4, core: 2. Of those that a mesh axis runs over, the one named last changes fastest.
Arguments:
- probes: bfloat16 [96, 128, 128], P('clus', 'probe'), may hold values from -6 to 6
- onsite: float32 [96, 128], P('clus'), may hold values from -1.1 to 1.1
- hopping: bfloat16 [20, 96, 128, 128], P(None, 'clus'), may hold values from -0.0390625 to 0.0390625
- block_col: int32 [20, 96], P(None, 'clus'), may hold values from -1 to 95, as said below
- atom_of: int32 [96, 128], P('clus'), may hold values from 0 to 31, as said below
- bond_dir: bfloat16 [3, 20, 96], P(None, None, 'clus'), may hold values from -1 to 1, as said below
- chemical_potential: float32 [1], replicated, may hold values from -0.3 to 0.3
Outputs:
- density: float32 [96, 128], P('clus')
- filling: float32 [1], replicated
- forces: float32 [3, 3072], P(None, 'clus')
The draws below stay inside these ranges and needn't reach their ends.
Inputs may be any that keep to these rules, and one draw needn't show every extreme that they name: `block_col`: -1 marks an empty slot. Slot (m, c) belongs to row cluster c; a live slot's column cluster lies within 12 clusters of c, and the live columns of one row cluster are distinct. In each aligned group of 12 row clusters the live slots are those with m under a count common to the group, either 20 or from 5 to 10, except columns that would fall outside the grid, which are empty. In some group, never the first or the last, every slot is live. `atom_of`: in each cluster every atom number appears for exactly four orbitals. `bond_dir`: the three components of each slot form a unit vector.
All inputs are finite; a program needn't handle non-finite values.
Results may differ from the reference program's by a relative error of at most 0.0011.
Values may be sent and summed in bfloat16 or wider, within the bound.
No kernel may reach another device: no remote copies, remote signals or barrier semaphores. Data moves between devices by JAX's collectives and lax.ppermute only.
A program may use at most 128 MiB of HBM per device.

```python
import jax
import jax.numpy as jnp
from jax import lax

CL_DEV = 12
BLOCK = 128
ATOMS = 32
NB_FULL = 20
REACH = 12
PROBE_VECTORS = 128
ORDER = 4
NCLUS = 96


def draw_onsite(key, part):
    position = (jnp.arange(NCLUS, dtype=jnp.float32)[:, None] + 0.5) / NCLUS
    profile = 0.45 - 0.9 * position
    rough = jnp.clip(0.25 * jax.random.normal(key, (NCLUS, BLOCK), jnp.float32), -0.6, 0.6)
    return (profile + rough).astype(jnp.float32)


def draw_block_col(key, part):
    groups = NCLUS // CL_DEV
    busy_key, count_key, shuffle_key = jax.random.split(key, 3)
    busy_group = jax.random.randint(busy_key, (), 1, groups - 1)
    counts = jax.random.randint(count_key, (groups,), NB_FULL // 4, NB_FULL // 2 + 1)
    counts = jnp.where(jnp.arange(groups) == busy_group, NB_FULL, counts)
    cluster_count = jnp.repeat(counts, CL_DEV)
    cluster_keys = jax.random.split(shuffle_key, NCLUS)

    def shuffle_one(sub_key):
        return jax.random.permutation(sub_key, 2 * REACH + 1)
    shuffled = jax.vmap(shuffle_one)(cluster_keys)
    offsets = shuffled[:, :NB_FULL] - REACH
    row_index = jnp.arange(NCLUS)[:, None]
    col_index = row_index + offsets
    slot_index = jnp.arange(NB_FULL)[None, :]
    live_slot = (slot_index < cluster_count[:, None]) & (col_index >= 0) & (col_index < NCLUS)
    return jnp.where(live_slot, col_index, -1).T.astype(jnp.int32)


def draw_atom_of(key, part):
    cluster_keys = jax.random.split(key, NCLUS)

    def shuffle_one(sub_key):
        return jax.random.permutation(sub_key, BLOCK) // (BLOCK // ATOMS)
    return jax.vmap(shuffle_one)(cluster_keys).astype(jnp.int32)


def draw_bond_dir(key, part):
    first_key, second_key = jax.random.split(key)
    azimuth = jax.random.uniform(first_key, (NB_FULL, NCLUS), jnp.float32, -jnp.pi, jnp.pi)
    height = jnp.tanh(jax.random.normal(second_key, (NB_FULL, NCLUS), jnp.float32))
    radial = jnp.sqrt(jnp.maximum(1.0 - height * height, 0.0))
    return jnp.stack([radial * jnp.cos(azimuth), radial * jnp.sin(azimuth), height]).astype(jnp.bfloat16)


def level_of(own_key, shape, pieces, low, largest):
    gain = 1.0
    for dim, blocks in pieces:
        draws = jax.random.uniform(jax.random.fold_in(jax.random.fold_in(own_key, 6), dim), (blocks,), jnp.float32, low / len(pieces), largest / len(pieces))
        gain = gain * jnp.repeat(jnp.exp(draws), shape[dim] // blocks).reshape((-1,) + (1,) * (len(shape) - 1 - dim))
    return gain


def noise(key, dims, width, limit, cuts=(), kind=jnp.bfloat16):
    loudness = level_of(key, dims, cuts, -0.22, 0.18) if cuts else 1.0
    values = jax.random.normal(key, dims, jnp.float32) * width * loudness
    return jnp.minimum(jnp.maximum(values, -limit), limit).astype(kind)


def setup_inputs(seed: int = 0) -> dict:
    keys = jax.random.split(jax.random.key(seed), 8)
    probes = noise(keys[0], (NCLUS, PROBE_VECTORS, BLOCK), 1.0, 6.0, ((0, 8), (1, 4)))
    onsite = draw_onsite(jax.random.fold_in(keys[7], 71), 0)
    hopping = noise(keys[2], (NB_FULL, NCLUS, BLOCK, BLOCK), (8 * BLOCK * NB_FULL) ** -0.5, 0.0390625, ((1, 8),))
    block_col = draw_block_col(jax.random.fold_in(keys[7], 71), 0)
    atom_of = draw_atom_of(jax.random.fold_in(keys[7], 71), 0)
    bond_dir = draw_bond_dir(jax.random.fold_in(keys[7], 71), 0)
    chemical_potential = jnp.clip(jax.random.uniform(keys[6], (1,), jnp.float32, -0.3, 0.3), -0.3, 0.3)
    return dict(probes=probes, onsite=onsite, hopping=hopping, block_col=block_col, atom_of=atom_of, bond_dir=bond_dir, chemical_potential=chemical_potential)


DECAY = 50.0
SMEARING_TEMP = 0.1
quad_nodes = 64


def expansion(chemical_potential, degree):
    node_index = jnp.arange(quad_nodes, dtype=jnp.float32)
    bond_angles = jnp.pi * (node_index + 0.5) / quad_nodes
    fermi_occupation = 1.0 / (1.0 + jnp.exp((jnp.cos(bond_angles) - chemical_potential) / SMEARING_TEMP))
    orders = jnp.arange(degree + 1, dtype=jnp.float32)
    cosines = jnp.cos(orders[:, None] * bond_angles[None, :])
    coeffs = (2.0 / quad_nodes) * jnp.sum(cosines * fermi_occupation[None, :], axis=1)
    return coeffs * jnp.where(orders == 0.0, 0.5, 1.0)


def reference(probes, onsite, hopping, block_col, atom_of, bond_dir, chemical_potential):
    live_mask = block_col >= 0
    masked = jnp.where(live_mask[:, :, None, None], hopping, jnp.zeros((), hopping.dtype))
    target_ids = jnp.where(live_mask, block_col, NCLUS).astype(jnp.int32)
    safe_ids = jnp.clip(block_col, 0, NCLUS - 1).astype(jnp.int32)
    highest = lax.Precision.HIGHEST

    def operate(vector_b):
        wide = vector_b.astype(jnp.float32)

        def single_slab(total, slab):
            blocks, gather_ids, targets = slab
            blocks_wide = blocks.astype(jnp.float32)
            picked = jnp.take(wide, gather_ids, axis=0)
            direct = jnp.einsum("cpj,cij->cpi", picked, blocks_wide, precision=highest)
            spread = jnp.einsum("cpi,cij->cpj", wide, blocks_wide, precision=highest)
            carried = jax.ops.segment_sum(spread, targets, num_segments=NCLUS + 1)[:NCLUS]
            return total + direct + carried, None

        total, unused = lax.scan(single_slab, jnp.zeros(wide.shape, jnp.float32), (masked, safe_ids, target_ids))
        return onsite[:, None, :] * wide + total

    coeffs = expansion(chemical_potential[0], ORDER)
    probe_wide = probes.astype(jnp.float32)
    previous = probe_wide
    current = operate(probes)
    fermi_vec = coeffs[0] * previous + coeffs[1] * current
    for term_index in range(2, ORDER + 1):
        following = 2.0 * operate(current.astype(jnp.bfloat16)) - previous
        fermi_vec = fermi_vec + coeffs[term_index] * following
        previous, current = current, following

    norm_sq = jnp.sum(probe_wide * probe_wide, axis=(0, 2))
    scale = (NCLUS * BLOCK) / (norm_sq * PROBE_VECTORS)
    density = jnp.sum(probe_wide * fermi_vec * scale[None, :, None], axis=1)
    filling = jnp.sum(density).reshape(1) / (NCLUS * BLOCK)
    weighted = (fermi_vec * scale[None, :, None]).astype(jnp.bfloat16)
    weighted_wide = weighted.astype(jnp.float32)
    facing_all = jnp.transpose(bond_dir.astype(jnp.float32), (1, 0, 2))

    def force_slab(total, slab):
        blocks, gather_ids, targets, facing = slab
        blocks_wide = blocks.astype(jnp.float32)
        u_cols = jnp.take(weighted_wide, gather_ids, axis=0)
        v_cols = jnp.take(probe_wide, gather_ids, axis=0)
        dens = jnp.einsum("cpi,cpj->cij", weighted_wide, v_cols, precision=highest)
        dens = dens + jnp.einsum("cpi,cpj->cij", probe_wide, u_cols, precision=highest)
        product = dens * blocks_wide
        row_sums = jnp.sum(product, axis=2)
        col_sums = jnp.sum(product, axis=1)
        turned = facing.T
        row_terms = -DECAY * turned[:, :, None] * row_sums[:, None, :]
        col_terms = DECAY * turned[:, :, None] * col_sums[:, None, :]
        moved = jax.ops.segment_sum(col_terms, targets, num_segments=NCLUS + 1)[:NCLUS]
        return total + row_terms + moved, None

    orbital_gradient, unused = lax.scan(force_slab, jnp.zeros((NCLUS, 3, BLOCK), jnp.float32), (masked, safe_ids, target_ids, facing_all))
    atom_table = (atom_of[:, :, None] == jnp.arange(ATOMS, dtype=jnp.int32)[None, None, :]).astype(jnp.float32)
    forces = jnp.einsum("cxb,cba->xca", orbital_gradient, atom_table, precision=highest).reshape(3, NCLUS * ATOMS)
    return density, filling, forces
```

```python
import functools

import jax
import jax.numpy as jnp
from jax import lax
from jax.experimental import pallas as pl
from jax.experimental.pallas import tpu as pltpu
from jax.sharding import PartitionSpec as P

ATOMS = 32
REACH = 12
PROBE_VECTORS = 128
ORDER = 4
DECAY = 50.0
SMEARING_TEMP = 0.1
QUAD_NODES = 64
HALF_SLOTS = 10

bf16 = jnp.bfloat16
f32 = jnp.float32
NN = (((1,), (0,)), ((), ()))
NT = (((1,), (1,)), ((), ()))
dot = functools.partial(lax.dot_general, preferred_element_type=f32)
VM = pl.BlockSpec(memory_space=pltpu.VMEM)
SM = pl.BlockSpec(memory_space=pltpu.SMEM)


def params(flops, nbytes):
    return dict(
        compiler_params=pltpu.CompilerParams(vmem_limit_bytes=8 << 20),
        cost_estimate=pl.CostEstimate(flops=flops, bytes_accessed=nbytes, transcendentals=0),
    )


def expansion(chemical_potential, degree):
    node_index = jnp.arange(QUAD_NODES, dtype=f32)
    bond_angles = jnp.pi * (node_index + 0.5) / QUAD_NODES
    fermi_occupation = 1.0 / (
        1.0 + jnp.exp((jnp.cos(bond_angles) - chemical_potential) / SMEARING_TEMP)
    )
    orders = jnp.arange(degree + 1, dtype=f32)
    cosines = jnp.cos(orders[:, None] * bond_angles[None, :])
    coeffs = 2.0 / QUAD_NODES * jnp.sum(cosines * fermi_occupation[None, :], axis=1)
    return coeffs * jnp.where(orders == 0.0, 0.5, 1.0)


def exchange(even_side, odd_side):
    count = lax.axis_size("clus")
    paired = [(i, i ^ 1) for i in range(count)]
    shifted = [(i, i + 1 if i % 2 else i - 1) for i in range(count)]
    shifted = [(i, j if 0 <= j < count else i) for i, j in shifted]
    crossed = lax.ppermute(odd_side, "clus", shifted)
    return lax.ppermute(even_side, "clus", paired), crossed


def doubled_sum(part, axis):
    step = 1
    while step < lax.axis_size(axis):
        pairs = [(i, i ^ step) for i in range(lax.axis_size(axis))]
        part = part + lax.ppermute(part, axis, pairs)
        step *= 2
    return part


def by_size(flag, slots, body):
    @pl.when(flag[0] != 0)
    def _():
        body(slots)

    @pl.when(flag[0] == 0)
    def _():
        body(HALF_SLOTS)


def spread(flag, ids, x, k):
    slots, rows, block, _ = k.shape
    probes = x.shape[1]
    frame = rows + 2 * REACH

    def kernel(turn, flag_ref, ids_ref, x_ref, k_ref, own_ref, even_ref, odd_ref, *rest):
        acc = rest[-1]
        acc[...] = jnp.zeros_like(acc)

        def body(count):
            for c in range(rows):
                xc = x_ref[c]
                for first in range(0, count, 4):
                    parts, targets = [], []
                    for m in range(first, min(first + 4, count), 2):
                        pair = [k_ref[m, c], k_ref[m + 1, c]]
                        out = dot(xc, jnp.concatenate(pair, axis=1), NN)
                        parts += [out[:, :block], out[:, block:]]
                        targets += [ids_ref[m, c], ids_ref[m + 1, c]]
                        if turn:
                            rest[0][m, c] = pair[0].T
                            rest[0][m + 1, c] = pair[1].T
                    values = [acc[t] + part for t, part in zip(targets, parts)]
                    for t, value in zip(targets, values):
                        acc[t] = value

        by_size(flag_ref, slots, body)
        odd = flag_ref[1]
        own_ref[...] = acc[pl.ds(REACH, rows)]
        even_ref[...] = acc[pl.ds((1 - odd) * (REACH + rows), REACH)].astype(bf16)
        odd_ref[...] = acc[pl.ds(odd * (REACH + rows), REACH)].astype(bf16)

    side = jax.ShapeDtypeStruct((REACH, probes, block), bf16)
    shapes = [jax.ShapeDtypeStruct((rows, probes, block), f32), side, side]

    def call(turn):
        out = shapes + ([jax.ShapeDtypeStruct(k.shape, k.dtype)] if turn else [])
        return pl.pallas_call(
            functools.partial(kernel, turn),
            out_shape=out,
            in_specs=[SM, SM, VM, VM],
            out_specs=[VM] * len(out),
            scratch_shapes=[pltpu.VMEM((frame + 1, probes, block), f32)],
            name="spread_turn" if turn else "spread",
            **params(2 * slots * rows * probes * block * block, k.size * 2),
        )(flag, ids, x, k)

    return call


def fill_frame(frame_ref, odd, own, even, crossed):
    rows = own.shape[0]
    frame_ref[pl.ds(REACH, rows)] = own[...]
    frame_ref[pl.ds((1 - odd) * (REACH + rows), REACH)] = even[...]
    frame_ref[pl.ds(odd * (REACH + rows), REACH)] = crossed[...]
    frame_ref[rows + 2 * REACH] = jnp.zeros(own.shape[1:], own.dtype)


def direct(flag, ids, x, even, crossed, kt, own, onsite):
    slots, rows, block, _ = kt.shape
    probes = x.shape[1]

    def kernel(flag_ref, ids_ref, x_ref, e_ref, o_ref, kt_ref, own_ref, site_ref, out_ref, frame):
        fill_frame(frame, flag_ref[1], x_ref, e_ref, o_ref)

        def body(count):
            for c in range(rows):
                acc = own_ref[c] + site_ref[pl.ds(c, 1)] * x_ref[c].astype(f32)
                for m in range(0, count, 2):
                    pair = [frame[ids_ref[m, c]], frame[ids_ref[m + 1, c]]]
                    weights = jnp.concatenate([kt_ref[m, c], kt_ref[m + 1, c]], axis=0)
                    acc = acc + dot(jnp.concatenate(pair, axis=1), weights, NN)
                out_ref[c] = acc

        by_size(flag_ref, slots, body)

    return pl.pallas_call(
        kernel,
        out_shape=jax.ShapeDtypeStruct((rows, probes, block), f32),
        in_specs=[SM, SM, VM, VM, VM, VM, VM, VM],
        out_specs=VM,
        scratch_shapes=[pltpu.VMEM((rows + 2 * REACH + 1, probes, block), bf16)],
        name="direct",
        **params(2 * slots * rows * probes * block * block, kt.size * 2),
    )(flag, ids, x, even, crossed, kt, own, onsite)


def images(flag, v, w, k):
    slots, rows, block, _ = k.shape
    probes = v.shape[1]

    def kernel(flag_ref, v_ref, w_ref, k_ref, out_ref):
        def body(count):
            for c in range(rows):
                left = jnp.concatenate([w_ref[c], v_ref[c]], axis=0)
                for m in range(0, count, 2):
                    out = dot(left, jnp.concatenate([k_ref[m, c], k_ref[m + 1, c]], axis=1), NN)
                    out_ref[m, c] = out[:, :block]
                    out_ref[m + 1, c] = out[:, block:]

        by_size(flag_ref, slots, body)

    return pl.pallas_call(
        kernel,
        out_shape=jax.ShapeDtypeStruct((slots, rows, 2 * probes, block), f32),
        in_specs=[SM, VM, VM, VM],
        out_specs=VM,
        name="images",
        **params(4 * slots * rows * probes * block * block, k.size * 2),
    )(flag, v, w, k)


def forces(flag, ids, bond, v, v_even, v_crossed, w, w_even, w_crossed, kt, image):
    slots, rows, block, _ = kt.shape
    probes = v.shape[1]
    frame_rows = rows + 2 * REACH
    sub = 8

    def folded(value):
        parts = [value[i : i + sub] for i in range(0, value.shape[0], sub)]
        while len(parts) > 1:
            parts = [a + b for a, b in zip(parts[::2], parts[1::2])]
        return parts[0]

    def kernel(flag_ref, ids_ref, bond_ref, *refs):
        v_ref, ve_ref, vo_ref, w_ref, we_ref, wo_ref, kt_ref, image_ref = refs[:8]
        own_ref, even_ref, odd_ref, vf, wf, acc = refs[8:]
        odd = flag_ref[1]
        fill_frame(vf, odd, v_ref, ve_ref, vo_ref)
        fill_frame(wf, odd, w_ref, we_ref, wo_ref)
        acc[...] = jnp.zeros_like(acc)

        def body(count):
            for c in range(rows):
                mine = jnp.concatenate([w_ref[c], v_ref[c]], axis=0).astype(f32)
                row = [jnp.zeros((sub, block), f32)] * 3
                for m in range(0, count, 2):
                    far = []
                    for slot in (m, m + 1):
                        d = ids_ref[slot, c]
                        far.append(jnp.concatenate([vf[d], wf[d]], axis=0))
                    weights = jnp.concatenate([kt_ref[m, c], kt_ref[m + 1, c]], axis=1)
                    out = dot(jnp.concatenate(far, axis=0), weights, NN)
                    direct_parts = [out[: 2 * probes, :block], out[2 * probes :, block:]]
                    for slot, other, part in zip((m, m + 1), far, direct_parts):
                        d = ids_ref[slot, c]
                        row_part = folded(mine * part)
                        col_part = folded(other.astype(f32) * image_ref[slot, c])
                        for axis in range(3):
                            b = bond_ref[axis * slots + slot, c]
                            row[axis] = row[axis] + b * row_part
                            acc[d, axis] = acc[d, axis] + b * col_part
                for axis in range(3):
                    acc[c + REACH, axis] = acc[c + REACH, axis] - row[axis]

        by_size(flag_ref, slots, body)

        def taken(start, count):
            return DECAY * jnp.sum(acc[pl.ds(start, count)], axis=2)

        own_ref[...] = taken(REACH, rows)
        even_ref[...] = taken((1 - odd) * (REACH + rows), REACH)
        odd_ref[...] = taken(odd * (REACH + rows), REACH)

    side = jax.ShapeDtypeStruct((REACH, 3, block), f32)
    frame = pltpu.VMEM((frame_rows + 1, probes, block), bf16)
    return pl.pallas_call(
        kernel,
        out_shape=[jax.ShapeDtypeStruct((rows, 3, block), f32), side, side],
        in_specs=[SM, SM, SM] + [VM] * 8,
        out_specs=[VM] * 3,
        scratch_shapes=[frame, frame, pltpu.VMEM((frame_rows + 1, 3, sub, block), f32)],
        name="forces",
        **params(4 * slots * rows * probes * block * block, kt.size * 2 + image.size * 4),
    )(flag, ids, bond, v, v_even, v_crossed, w, w_even, w_crossed, kt, image)


def local(probes, onsite, hopping, block_col, atom_of, bond_dir, chemical_potential):
    rows, _, block = probes.shape
    slots = hopping.shape[0]
    me = lax.axis_index("clus")
    orbitals = rows * lax.axis_size("clus") * block
    live = block_col >= 0
    ids = jnp.where(live, block_col - me * rows + REACH, rows + 2 * REACH)
    many = jnp.max(block_col[HALF_SLOTS:]) >= 0
    flag = jnp.stack([many.astype(jnp.int32), (me % 2).astype(jnp.int32)])
    bond = bond_dir.astype(f32).reshape(3 * slots, rows)

    x = probes
    even, crossed = exchange(x, x)
    v_even, v_crossed = even, crossed
    wide = probes.astype(f32)
    square = doubled_sum(jnp.sum(wide * wide, axis=0), "clus")
    scale = orbitals / (jnp.sum(square, axis=1) * PROBE_VECTORS)
    coeffs = expansion(chemical_potential[0], ORDER)

    cheb = [wide]
    for term in range(1, ORDER + 1):
        outs = spread(flag, ids, x, hopping)(term == 1)
        if term == 1:
            turned = outs[3]
        back_even, back_crossed = exchange(outs[1], outs[2])
        image = direct(flag, ids, x, even, crossed, turned, outs[0], onsite)
        image = image + (back_even.astype(f32) + back_crossed.astype(f32))
        cheb.append(image if term == 1 else 2.0 * image - cheb[-2])
        x = cheb[-1].astype(bf16)
        if term < ORDER:
            even, crossed = exchange(x, x)
    fermi = coeffs[0] * cheb[0]
    for term in range(1, ORDER + 1):
        fermi = fermi + coeffs[term] * cheb[term]
    scaled = fermi * scale[None, :, None]
    density_part = jnp.sum(wide * scaled, axis=1)
    weighted = scaled.astype(bf16)
    w_even, w_crossed = exchange(weighted, weighted)
    image = images(flag, probes, weighted, hopping)
    filled = doubled_sum(jnp.sum(density_part, axis=0, keepdims=True), "clus")
    own, to_even, to_odd = forces(
        flag, ids, bond, probes, v_even, v_crossed, weighted, w_even, w_crossed, turned, image
    )
    from_even, from_odd = exchange(to_even, to_odd)
    gradient = own + from_even + from_odd
    atom_table = (atom_of[:, :, None] == jnp.arange(ATOMS, dtype=jnp.int32)[None, None, :]).astype(f32)
    atom_part = jnp.einsum(
        "rxb,rba->xra", gradient, atom_table, precision=lax.Precision.HIGHEST
    ).reshape(-1, block)
    packed = jnp.concatenate([density_part, atom_part, filled], axis=0)
    total = packed
    count = lax.axis_size("probe")
    for step in range(1, count):
        total = total + lax.ppermute(packed, "probe", [(i, (i + step) % count) for i in range(count)])
    density = total[:rows]
    atom_force = total[rows:-1].reshape(3, -1)
    filling = jnp.sum(total[-1]) / orbitals
    return (density, filling.reshape(1), atom_force)


def solution(mesh):
    placed = (
        P("clus", "probe", None),
        P("clus", None),
        P(None, "clus", None, None),
        P(None, "clus"),
        P("clus", None),
        P(None, None, "clus"),
        P(),
    )
    return jax.shard_map(
        local,
        mesh=mesh,
        in_specs=placed,
        out_specs=(P("clus", None), P(), P(None, "clus")),
        check_vma=False,
    )
```

```python
import functools

import jax
import jax.numpy as jnp
import numpy as np
from jax import lax
from jax.experimental import pallas as pl
from jax.experimental.pallas import tpu as pltpu
from jax.sharding import PartitionSpec as P

ATOMS = 32
REACH = 12
PROBE_VECTORS = 128
ORDER = 4
DECAY = 50.0
SMEARING_TEMP = 0.1
QUAD_NODES = 64
HALF_SLOTS = 10

bf16 = jnp.bfloat16
f32 = jnp.float32
NN = (((1,), (0,)), ((), ()))
NT = (((1,), (1,)), ((), ()))
dot = functools.partial(lax.dot_general, preferred_element_type=f32)
VM = pl.BlockSpec(memory_space=pltpu.VMEM)
SM = pl.BlockSpec(memory_space=pltpu.SMEM)


def params(flops, nbytes):
    return dict(
        compiler_params=pltpu.CompilerParams(vmem_limit_bytes=8 << 20),
        cost_estimate=pl.CostEstimate(flops=flops, bytes_accessed=nbytes, transcendentals=0),
    )


def quadrature():
    angles = np.pi * (np.arange(QUAD_NODES) + 0.5) / QUAD_NODES
    table = np.zeros((8, 128), np.float32)
    for order in range(ORDER + 1):
        weight = 2.0 / QUAD_NODES * (0.5 if order == 0 else 1.0)
        table[order, :QUAD_NODES] = weight * np.cos(order * angles)
    table[7, :QUAD_NODES] = np.cos(angles)
    return jnp.asarray(table)


def prepared(columns, bond_dir, chemical_potential):
    rows, slots = columns.shape

    def kernel(col_ref, bond_ref, mu_ref, table_ref, flag_ref, ids_ref, out_ref, coeff_ref):
        me = lax.axis_index("clus")
        col = col_ref[...]
        ids_ref[...] = jnp.where(col >= 0, col - me * rows + REACH, rows + 2 * REACH)
        late = lax.broadcasted_iota(jnp.int32, col.shape, 1) >= HALF_SLOTS
        flag_ref[0] = (jnp.max(jnp.where(late, col, -1)) >= 0).astype(jnp.int32)
        flag_ref[1] = lax.rem(me, 2)
        for axis in range(3):
            out_ref[axis * rows : (axis + 1) * rows] = bond_ref[axis].astype(f32)
        energy = (table_ref[7:8] - mu_ref[0]) / SMEARING_TEMP
        occupied = 1.0 / (1.0 + jnp.exp(energy))
        total = jnp.sum(table_ref[...] * occupied, axis=1, keepdims=True)
        coeff_ref[...] = jnp.broadcast_to(total, coeff_ref.shape)

    return pl.pallas_call(
        kernel,
        out_shape=[
            jax.ShapeDtypeStruct((2,), jnp.int32),
            jax.ShapeDtypeStruct((rows, slots), jnp.int32),
            jax.ShapeDtypeStruct((3 * rows, slots), f32),
            jax.ShapeDtypeStruct((8, 128), f32),
        ],
        in_specs=[VM, VM, SM, VM],
        out_specs=[SM, VM, VM, VM],
        name="prepared",
        **params(1000, 50000),
    )(columns, bond_dir, chemical_potential, quadrature())


def moments(coeffs, v, first, second):
    _, probes, block = v.shape

    def kernel(coeff_ref, v_ref, a_ref, b_ref, out_ref):
        wide = v_ref[...].astype(f32)
        a, b = a_ref[...], b_ref[...]
        pairs = (wide * wide, wide * a, wide * b, a * b, b * b)
        m0, m1, m2, ab, bb = [jnp.sum(pair, axis=0) for pair in pairs]
        c = [coeff_ref[k : k + 1] for k in range(ORDER + 1)]
        out_ref[0] = m0
        out_ref[1] = (
            c[0] * m0 + c[1] * m1 + c[2] * m2 + c[3] * (2.0 * ab - m1) + c[4] * (2.0 * bb - m0)
        )

    return pl.pallas_call(
        kernel,
        out_shape=jax.ShapeDtypeStruct((2, probes, block), f32),
        in_specs=[VM] * 4,
        out_specs=VM,
        name="moments",
        **params(10 * v.size, 10 * v.size),
    )(coeffs, v, first, second)


def closed(coeffs, sums, orbitals, cheb, image, back_even, back_crossed):
    rows, probes, block = image.shape

    def kernel(coeff_ref, sum_ref, c0, c1, c2, c3, y_ref, e_ref, o_ref, w_ref, head_ref):
        square = jnp.sum(sum_ref[0], axis=1, keepdims=True)
        scale = orbitals / (square * PROBE_VECTORS)
        head_ref[...] = jnp.zeros_like(head_ref)
        head_ref[rows : rows + 1] = jnp.sum(scale * sum_ref[1], axis=0, keepdims=True)
        scale = jnp.broadcast_to(scale, (probes, block))
        c = [coeff_ref[k : k + 1] for k in range(ORDER + 1)]
        for r in range(rows):
            y = y_ref[r] + (e_ref[r].astype(f32) + o_ref[r].astype(f32))
            wide = c0[r].astype(f32)
            fermi = c[0] * wide + c[1] * c1[r]
            fermi = fermi + c[2] * c2[r]
            fermi = fermi + c[3] * c3[r]
            fermi = fermi + c[4] * (2.0 * y - c2[r])
            scaled = fermi * scale
            w_ref[r] = scaled.astype(bf16)
            head_ref[r : r + 1] = jnp.sum(wide * scaled, axis=0, keepdims=True)

    return pl.pallas_call(
        kernel,
        out_shape=[
            jax.ShapeDtypeStruct((rows, probes, block), bf16),
            jax.ShapeDtypeStruct((16, block), f32),
        ],
        in_specs=[VM] * 9,
        out_specs=[VM] * 2,
        name="closed",
        **params(20 * image.size, 30 * image.size),
    )(coeffs, sums, *cheb, image, back_even, back_crossed)


def packed(head, own, from_even, from_odd, atom_of):
    rows, _, block = own.shape
    group = block // ATOMS
    lines = rows // group

    def kernel(head_ref, own_ref, e_ref, o_ref, atom_ref, out_ref):
        out_ref[...] = jnp.zeros_like(out_ref)
        out_ref[: rows + 1] = head_ref[: rows + 1]
        lane = lax.broadcasted_iota(jnp.int32, (block, block), 0)
        for line in range(lines):
            total = jnp.zeros((16, block), f32)
            for part in range(group):
                r = line * group + part
                g = own_ref[r] + e_ref[r] + o_ref[r]
                high = g.astype(bf16)
                rest = g - high.astype(f32)
                middle = rest.astype(bf16)
                low = (rest - middle.astype(f32)).astype(bf16)
                pad = jnp.zeros((16 - 9, block), bf16)
                left = jnp.concatenate([high, middle, low, pad], axis=0)
                hot = (lane == atom_ref[r : r + 1] + part * ATOMS).astype(f32).astype(bf16)
                total = total + dot(left, hot, NT)
            value = total[0:3] + (total[3:6] + total[6:9])
            for axis in range(3):
                at = rows + 1 + axis * lines + line
                out_ref[at : at + 1] = value[axis : axis + 1]

    height = -(-(rows + 1 + 3 * lines) // 8) * 8
    return pl.pallas_call(
        kernel,
        out_shape=jax.ShapeDtypeStruct((height, block), f32),
        in_specs=[VM] * 5,
        out_specs=VM,
        name="packed",
        **params(2 * rows * 16 * block * block, 100000),
    )(head, own, from_even, from_odd, atom_of)


def unpacked(parts, rows, orbitals):
    height, block = parts[0].shape
    lines = rows * ATOMS // block

    def kernel(*refs):
        ins, (density_ref, filling_ref, force_ref) = refs[: len(parts)], refs[len(parts) :]
        total = ins[0][...]
        for other in ins[1:]:
            total = total + other[...]
        density_ref[...] = total[:rows]
        filling_ref[0] = jnp.sum(total[rows : rows + 1]) / orbitals
        for axis in range(3):
            for line in range(lines):
                at = rows + 1 + axis * lines + line
                force_ref[axis : axis + 1, line * block : (line + 1) * block] = total[at : at + 1]

    return pl.pallas_call(
        kernel,
        out_shape=[
            jax.ShapeDtypeStruct((rows, block), f32),
            jax.ShapeDtypeStruct((1,), f32),
            jax.ShapeDtypeStruct((3, lines * block), f32),
        ],
        in_specs=[VM] * len(parts),
        out_specs=[VM, SM, VM],
        name="unpacked",
        **params(10000, 100000),
    )(*parts)


def exchange(even_side, odd_side):
    count = lax.axis_size("clus")
    paired = [(i, i ^ 1) for i in range(count)]
    shifted = [(i, i + 1 if i % 2 else i - 1) for i in range(count)]
    shifted = [(i, j if 0 <= j < count else i) for i, j in shifted]
    crossed = lax.ppermute(odd_side, "clus", shifted)
    return lax.ppermute(even_side, "clus", paired), crossed


def doubled_sum(part, axis):
    step = 1
    while step < lax.axis_size(axis):
        pairs = [(i, i ^ step) for i in range(lax.axis_size(axis))]
        part = part + lax.ppermute(part, axis, pairs)
        step *= 2
    return part


def by_size(flag, slots, body):
    @pl.when(flag[0] != 0)
    def _():
        body(slots)

    @pl.when(flag[0] == 0)
    def _():
        body(HALF_SLOTS)


def spread(flag, ids, x, k):
    slots, rows, block, _ = k.shape
    probes = x.shape[1]
    frame = rows + 2 * REACH

    def kernel(turn, flag_ref, ids_ref, x_ref, k_ref, own_ref, even_ref, odd_ref, *rest):
        acc = rest[-1]
        acc[...] = jnp.zeros_like(acc)

        def body(count):
            for c in range(rows):
                xc = x_ref[c]
                for first in range(0, count, 4):
                    parts, targets = [], []
                    for m in range(first, min(first + 4, count), 2):
                        pair = [k_ref[m, c], k_ref[m + 1, c]]
                        out = dot(xc, jnp.concatenate(pair, axis=1), NN)
                        parts += [out[:, :block], out[:, block:]]
                        targets += [ids_ref[c, m], ids_ref[c, m + 1]]
                        if turn:
                            rest[0][m, c] = pair[0].T
                            rest[0][m + 1, c] = pair[1].T
                    values = [acc[t] + part for t, part in zip(targets, parts)]
                    for t, value in zip(targets, values):
                        acc[t] = value

        by_size(flag_ref, slots, body)
        odd = flag_ref[1]
        own_ref[...] = acc[pl.ds(REACH, rows)]
        even_ref[...] = acc[pl.ds((1 - odd) * (REACH + rows), REACH)].astype(bf16)
        odd_ref[...] = acc[pl.ds(odd * (REACH + rows), REACH)].astype(bf16)

    side = jax.ShapeDtypeStruct((REACH, probes, block), bf16)
    shapes = [jax.ShapeDtypeStruct((rows, probes, block), f32), side, side]

    def call(turn):
        out = shapes + ([jax.ShapeDtypeStruct(k.shape, k.dtype)] if turn else [])
        return pl.pallas_call(
            functools.partial(kernel, turn),
            out_shape=out,
            in_specs=[SM, SM, VM, VM],
            out_specs=[VM] * len(out),
            scratch_shapes=[pltpu.VMEM((frame + 1, probes, block), f32)],
            name="spread_turn" if turn else "spread",
            **params(2 * slots * rows * probes * block * block, k.size * 2),
        )(flag, ids, x, k)

    return call


def fill_frame(frame_ref, odd, own, even, crossed):
    rows = own.shape[0]
    frame_ref[pl.ds(REACH, rows)] = own[...]
    frame_ref[pl.ds((1 - odd) * (REACH + rows), REACH)] = even[...]
    frame_ref[pl.ds(odd * (REACH + rows), REACH)] = crossed[...]
    frame_ref[rows + 2 * REACH] = jnp.zeros(own.shape[1:], own.dtype)


def direct(flag, ids, x, even, crossed, kt, own, onsite):
    slots, rows, block, _ = kt.shape
    probes = x.shape[1]

    def kernel(flag_ref, ids_ref, x_ref, e_ref, o_ref, kt_ref, own_ref, site_ref, out_ref, frame):
        fill_frame(frame, flag_ref[1], x_ref, e_ref, o_ref)

        def body(count):
            for c in range(rows):
                acc = own_ref[c] + site_ref[pl.ds(c, 1)] * x_ref[c].astype(f32)
                for m in range(0, count, 2):
                    pair = [frame[ids_ref[c, m]], frame[ids_ref[c, m + 1]]]
                    weights = jnp.concatenate([kt_ref[m, c], kt_ref[m + 1, c]], axis=0)
                    acc = acc + dot(jnp.concatenate(pair, axis=1), weights, NN)
                out_ref[c] = acc

        by_size(flag_ref, slots, body)

    return pl.pallas_call(
        kernel,
        out_shape=jax.ShapeDtypeStruct((rows, probes, block), f32),
        in_specs=[SM, SM, VM, VM, VM, VM, VM, VM],
        out_specs=VM,
        scratch_shapes=[pltpu.VMEM((rows + 2 * REACH + 1, probes, block), bf16)],
        name="direct",
        **params(2 * slots * rows * probes * block * block, kt.size * 2),
    )(flag, ids, x, even, crossed, kt, own, onsite)


def images(flag, v, w, k):
    slots, rows, block, _ = k.shape
    probes = v.shape[1]

    def kernel(flag_ref, v_ref, w_ref, k_ref, out_ref):
        def body(count):
            for c in range(rows):
                left = jnp.concatenate([w_ref[c], v_ref[c]], axis=0)
                for m in range(0, count, 2):
                    out = dot(left, jnp.concatenate([k_ref[m, c], k_ref[m + 1, c]], axis=1), NN)
                    out_ref[m, c] = out[:, :block]
                    out_ref[m + 1, c] = out[:, block:]

        by_size(flag_ref, slots, body)

    return pl.pallas_call(
        kernel,
        out_shape=jax.ShapeDtypeStruct((slots, rows, 2 * probes, block), f32),
        in_specs=[SM, VM, VM, VM],
        out_specs=VM,
        name="images",
        **params(4 * slots * rows * probes * block * block, k.size * 2),
    )(flag, v, w, k)


def forces(flag, ids, bond, v, v_even, v_crossed, w, w_even, w_crossed, kt, image):
    slots, rows, block, _ = kt.shape
    probes = v.shape[1]
    frame_rows = rows + 2 * REACH
    sub = 8

    def folded(value):
        parts = [value[i : i + sub] for i in range(0, value.shape[0], sub)]
        while len(parts) > 1:
            parts = [a + b for a, b in zip(parts[::2], parts[1::2])]
        return parts[0]

    def kernel(flag_ref, ids_ref, bond_ref, *refs):
        v_ref, ve_ref, vo_ref, w_ref, we_ref, wo_ref, kt_ref, image_ref = refs[:8]
        own_ref, even_ref, odd_ref, vf, wf, acc = refs[8:]
        odd = flag_ref[1]
        fill_frame(vf, odd, v_ref, ve_ref, vo_ref)
        fill_frame(wf, odd, w_ref, we_ref, wo_ref)
        acc[...] = jnp.zeros_like(acc)

        def body(count):
            for c in range(rows):
                mine = jnp.concatenate([w_ref[c], v_ref[c]], axis=0).astype(f32)
                row = [jnp.zeros((sub, block), f32)] * 3
                for m in range(0, count, 2):
                    far = []
                    for slot in (m, m + 1):
                        d = ids_ref[c, slot]
                        far.append(jnp.concatenate([vf[d], wf[d]], axis=0))
                    weights = jnp.concatenate([kt_ref[m, c], kt_ref[m + 1, c]], axis=1)
                    out = dot(jnp.concatenate(far, axis=0), weights, NN)
                    direct_parts = [out[: 2 * probes, :block], out[2 * probes :, block:]]
                    for slot, other, part in zip((m, m + 1), far, direct_parts):
                        d = ids_ref[c, slot]
                        row_part = folded(mine * part)
                        col_part = folded(other.astype(f32) * image_ref[slot, c])
                        for axis in range(3):
                            b = bond_ref[axis * rows + c, slot]
                            row[axis] = row[axis] + b * row_part
                            acc[d, axis] = acc[d, axis] + b * col_part
                for axis in range(3):
                    acc[c + REACH, axis] = acc[c + REACH, axis] - row[axis]

        by_size(flag_ref, slots, body)

        def taken(start, count):
            return DECAY * jnp.sum(acc[pl.ds(start, count)], axis=2)

        own_ref[...] = taken(REACH, rows)
        even_ref[...] = taken((1 - odd) * (REACH + rows), REACH)
        odd_ref[...] = taken(odd * (REACH + rows), REACH)

    side = jax.ShapeDtypeStruct((REACH, 3, block), f32)
    frame = pltpu.VMEM((frame_rows + 1, probes, block), bf16)
    return pl.pallas_call(
        kernel,
        out_shape=[jax.ShapeDtypeStruct((rows, 3, block), f32), side, side],
        in_specs=[SM, SM, SM] + [VM] * 8,
        out_specs=[VM] * 3,
        scratch_shapes=[frame, frame, pltpu.VMEM((frame_rows + 1, 3, sub, block), f32)],
        name="forces",
        **params(4 * slots * rows * probes * block * block, kt.size * 2 + image.size * 4),
    )(flag, ids, bond, v, v_even, v_crossed, w, w_even, w_crossed, kt, image)


def local(probes, onsite, hopping, block_col, atom_of, bond_dir, chemical_potential):
    rows, _, block = probes.shape
    orbitals = float(rows * lax.axis_size("clus") * block)
    flag, ids, bond, coeffs = prepared(
        block_col.T, jnp.transpose(bond_dir, (0, 2, 1)), chemical_potential
    )
    x = probes
    even, crossed = exchange(x, x)
    v_even, v_crossed = even, crossed
    cheb = [probes]
    for term in range(1, ORDER + 1):
        outs = spread(flag, ids, x, hopping)(term == 1)
        if term == 1:
            turned = outs[3]
        back_even, back_crossed = exchange(outs[1], outs[2])
        image = direct(flag, ids, x, even, crossed, turned, outs[0], onsite)
        if term == ORDER:
            break
        image = image + (back_even.astype(f32) + back_crossed.astype(f32))
        cheb.append(image if term == 1 else 2.0 * image - cheb[-2].astype(f32))
        x = cheb[-1].astype(bf16)
        even, crossed = exchange(x, x)
        if term == 2:
            sums = doubled_sum(moments(coeffs, *cheb), "clus")
    weighted, head = closed(coeffs, sums, orbitals, cheb, image, back_even, back_crossed)
    w_even, w_crossed = exchange(weighted, weighted)
    image = images(flag, probes, weighted, hopping)
    own, to_even, to_odd = forces(
        flag, ids, bond, probes, v_even, v_crossed, weighted, w_even, w_crossed, turned, image
    )
    from_even, from_odd = exchange(to_even, to_odd)
    part = packed(head, own, from_even, from_odd, atom_of)
    count = lax.axis_size("probe")
    parts = [part]
    step = 1
    while step < count:
        part = sum(parts[1:], parts[0])
        parts = [part, lax.ppermute(part, "probe", [(i, i ^ step) for i in range(count)])]
        step *= 2
    return tuple(unpacked(parts, rows, orbitals))


def solution(mesh):
    placed = (
        P("clus", "probe", None),
        P("clus", None),
        P(None, "clus", None, None),
        P(None, "clus"),
        P("clus", None),
        P(None, None, "clus"),
        P(),
    )
    return jax.shard_map(
        local,
        mesh=mesh,
        in_specs=placed,
        out_specs=(P("clus", None), P(), P(None, "clus")),
        check_vma=False,
    )
```

```python
import functools

import jax
import jax.numpy as jnp
import numpy as np
from jax import lax
from jax.experimental import pallas as pl
from jax.experimental.pallas import tpu as pltpu
from jax.sharding import PartitionSpec as P

ATOMS = 32
REACH = 12
PROBE_VECTORS = 128
ORDER = 4
DECAY = 50.0
SMEARING_TEMP = 0.1
QUAD_NODES = 64
HALF_SLOTS = 10

bf16 = jnp.bfloat16
f32 = jnp.float32
NN = (((1,), (0,)), ((), ()))
NT = (((1,), (1,)), ((), ()))
dot = functools.partial(lax.dot_general, preferred_element_type=f32)
VM = pl.BlockSpec(memory_space=pltpu.VMEM)
SM = pl.BlockSpec(memory_space=pltpu.SMEM)


def params(flops, nbytes):
    return dict(
        compiler_params=pltpu.CompilerParams(vmem_limit_bytes=8 << 20),
        cost_estimate=pl.CostEstimate(flops=flops, bytes_accessed=nbytes, transcendentals=0),
    )


def quadrature():
    angles = np.pi * (np.arange(QUAD_NODES) + 0.5) / QUAD_NODES
    table = np.zeros((8, 128), np.float32)
    for order in range(ORDER + 1):
        weight = 2.0 / QUAD_NODES * (0.5 if order == 0 else 1.0)
        table[order, :QUAD_NODES] = weight * np.cos(order * angles)
    table[7, :QUAD_NODES] = np.cos(angles)
    return jnp.asarray(table)


def prepared(columns, bond_dir, chemical_potential):
    rows, slots = columns.shape

    def kernel(col_ref, bond_ref, mu_ref, table_ref, flag_ref, ids_ref, out_ref, coeff_ref):
        me = lax.axis_index("clus")
        col = col_ref[...]
        ids_ref[...] = jnp.where(col >= 0, col - me * rows + REACH, rows + 2 * REACH)
        late = lax.broadcasted_iota(jnp.int32, col.shape, 1) >= HALF_SLOTS
        flag_ref[0] = (jnp.max(jnp.where(late, col, -1)) >= 0).astype(jnp.int32)
        flag_ref[1] = lax.rem(me, 2)
        for axis in range(3):
            out_ref[axis * rows : (axis + 1) * rows] = bond_ref[axis].astype(f32)
        energy = (table_ref[7:8] - mu_ref[0]) / SMEARING_TEMP
        occupied = 1.0 / (1.0 + jnp.exp(energy))
        total = jnp.sum(table_ref[...] * occupied, axis=1, keepdims=True)
        coeff_ref[...] = jnp.broadcast_to(total, coeff_ref.shape)

    return pl.pallas_call(
        kernel,
        out_shape=[
            jax.ShapeDtypeStruct((2,), jnp.int32),
            jax.ShapeDtypeStruct((rows, slots), jnp.int32),
            jax.ShapeDtypeStruct((3 * rows, slots), f32),
            jax.ShapeDtypeStruct((8, 128), f32),
        ],
        in_specs=[VM, VM, SM, VM],
        out_specs=[SM, VM, VM, VM],
        name="prepared",
        **params(1000, 50000),
    )(columns, bond_dir, chemical_potential, quadrature())


def moments(coeffs, v, first, second):
    _, probes, block = v.shape

    def kernel(coeff_ref, v_ref, a_ref, b_ref, out_ref):
        wide = v_ref[...].astype(f32)
        a, b = a_ref[...], b_ref[...]
        pairs = (wide * wide, wide * a, wide * b, a * b, b * b)
        m0, m1, m2, ab, bb = [jnp.sum(pair, axis=0) for pair in pairs]
        c = [coeff_ref[k : k + 1] for k in range(ORDER + 1)]
        out_ref[0] = m0
        out_ref[1] = (
            c[0] * m0 + c[1] * m1 + c[2] * m2 + c[3] * (2.0 * ab - m1) + c[4] * (2.0 * bb - m0)
        )

    return pl.pallas_call(
        kernel,
        out_shape=jax.ShapeDtypeStruct((2, probes, block), f32),
        in_specs=[VM] * 4,
        out_specs=VM,
        name="moments",
        **params(10 * v.size, 10 * v.size),
    )(coeffs, v, first, second)


def closed(coeffs, sums, orbitals, cheb, image, back_even, back_crossed):
    rows, probes, block = image.shape

    def kernel(coeff_ref, sum_ref, c0, c1, c2, c3, y_ref, e_ref, o_ref, w_ref, head_ref):
        square = jnp.sum(sum_ref[0], axis=1, keepdims=True)
        scale = orbitals / (square * PROBE_VECTORS)
        head_ref[...] = jnp.zeros_like(head_ref)
        head_ref[rows : rows + 1] = jnp.sum(scale * sum_ref[1], axis=0, keepdims=True)
        scale = jnp.broadcast_to(scale, (probes, block))
        c = [coeff_ref[k : k + 1] for k in range(ORDER + 1)]
        for r in range(rows):
            y = y_ref[r] + (e_ref[r].astype(f32) + o_ref[r].astype(f32))
            wide = c0[r].astype(f32)
            fermi = c[0] * wide + c[1] * c1[r]
            fermi = fermi + c[2] * c2[r]
            fermi = fermi + c[3] * c3[r]
            fermi = fermi + c[4] * (2.0 * y - c2[r])
            scaled = fermi * scale
            w_ref[r] = scaled.astype(bf16)
            head_ref[r : r + 1] = jnp.sum(wide * scaled, axis=0, keepdims=True)

    return pl.pallas_call(
        kernel,
        out_shape=[
            jax.ShapeDtypeStruct((rows, probes, block), bf16),
            jax.ShapeDtypeStruct((16, block), f32),
        ],
        in_specs=[VM] * 9,
        out_specs=[VM] * 2,
        name="closed",
        **params(20 * image.size, 30 * image.size),
    )(coeffs, sums, *cheb, image, back_even, back_crossed)


def packed(head, own, from_even, from_odd, atom_of):
    rows, _, block = own.shape
    group = block // ATOMS
    lines = rows // group

    def kernel(head_ref, own_ref, e_ref, o_ref, atom_ref, out_ref):
        out_ref[...] = jnp.zeros_like(out_ref)
        out_ref[: rows + 1] = head_ref[: rows + 1]
        lane = lax.broadcasted_iota(jnp.int32, (block, block), 0)
        for line in range(lines):
            total = jnp.zeros((16, block), f32)
            for part in range(group):
                r = line * group + part
                g = own_ref[r] + e_ref[r] + o_ref[r]
                high = g.astype(bf16)
                rest = g - high.astype(f32)
                middle = rest.astype(bf16)
                low = (rest - middle.astype(f32)).astype(bf16)
                pad = jnp.zeros((16 - 9, block), bf16)
                left = jnp.concatenate([high, middle, low, pad], axis=0)
                hot = (lane == atom_ref[r : r + 1] + part * ATOMS).astype(f32).astype(bf16)
                total = total + dot(left, hot, NT)
            value = total[0:3] + (total[3:6] + total[6:9])
            for axis in range(3):
                at = rows + 1 + axis * lines + line
                out_ref[at : at + 1] = value[axis : axis + 1]

    height = -(-(rows + 1 + 3 * lines) // 8) * 8
    return pl.pallas_call(
        kernel,
        out_shape=jax.ShapeDtypeStruct((height, block), f32),
        in_specs=[VM] * 5,
        out_specs=VM,
        name="packed",
        **params(2 * rows * 16 * block * block, 100000),
    )(head, own, from_even, from_odd, atom_of)


def unpacked(parts, rows, orbitals):
    height, block = parts[0].shape
    lines = rows * ATOMS // block

    def kernel(*refs):
        ins, (density_ref, filling_ref, force_ref) = refs[: len(parts)], refs[len(parts) :]
        total = ins[0][...]
        for other in ins[1:]:
            total = total + other[...]
        density_ref[...] = total[:rows]
        filling_ref[0] = jnp.sum(total[rows : rows + 1]) / orbitals
        for axis in range(3):
            for line in range(lines):
                at = rows + 1 + axis * lines + line
                force_ref[axis : axis + 1, line * block : (line + 1) * block] = total[at : at + 1]

    return pl.pallas_call(
        kernel,
        out_shape=[
            jax.ShapeDtypeStruct((rows, block), f32),
            jax.ShapeDtypeStruct((1,), f32),
            jax.ShapeDtypeStruct((3, lines * block), f32),
        ],
        in_specs=[VM] * len(parts),
        out_specs=[VM, SM, VM],
        name="unpacked",
        **params(10000, 100000),
    )(*parts)


def exchange(even_side, odd_side):
    count = lax.axis_size("clus")
    paired = [(i, i ^ 1) for i in range(count)]
    shifted = [(i, (i + 1 if i % 2 else i - 1) % count) for i in range(count)]
    crossed = lax.ppermute(odd_side, "clus", shifted)
    return lax.ppermute(even_side, "clus", paired), crossed


def doubled_sum(part, axis):
    step = 1
    while step < lax.axis_size(axis):
        pairs = [(i, i ^ step) for i in range(lax.axis_size(axis))]
        part = part + lax.ppermute(part, axis, pairs)
        step *= 2
    return part


def by_size(flag, slots, body):
    @pl.when(flag[0] != 0)
    def _():
        body(slots)

    @pl.when(flag[0] == 0)
    def _():
        body(HALF_SLOTS)


def spread(flag, ids, x, k):
    slots, rows, block, _ = k.shape
    probes = x.shape[1]
    frame = rows + 2 * REACH

    def kernel(turn, flag_ref, ids_ref, x_ref, k_ref, own_ref, even_ref, odd_ref, *rest):
        acc = rest[-1]
        acc[...] = jnp.zeros_like(acc)

        def body(count):
            for c in range(rows):
                xc = x_ref[c]
                for first in range(0, count, 4):
                    parts, targets = [], []
                    for m in range(first, min(first + 4, count), 2):
                        pair = [k_ref[m, c], k_ref[m + 1, c]]
                        out = dot(xc, jnp.concatenate(pair, axis=1), NN)
                        parts += [out[:, :block], out[:, block:]]
                        targets += [ids_ref[c, m], ids_ref[c, m + 1]]
                        if turn:
                            rest[0][m, c] = pair[0].T
                            rest[0][m + 1, c] = pair[1].T
                    values = [acc[t] + part for t, part in zip(targets, parts)]
                    for t, value in zip(targets, values):
                        acc[t] = value

        by_size(flag_ref, slots, body)
        odd = flag_ref[1]
        own_ref[...] = acc[pl.ds(REACH, rows)]
        even_ref[...] = acc[pl.ds((1 - odd) * (REACH + rows), REACH)].astype(bf16)
        odd_ref[...] = acc[pl.ds(odd * (REACH + rows), REACH)].astype(bf16)

    side = jax.ShapeDtypeStruct((REACH, probes, block), bf16)
    shapes = [jax.ShapeDtypeStruct((rows, probes, block), f32), side, side]

    def call(turn):
        out = shapes + ([jax.ShapeDtypeStruct(k.shape, k.dtype)] if turn else [])
        return pl.pallas_call(
            functools.partial(kernel, turn),
            out_shape=out,
            in_specs=[SM, SM, VM, VM],
            out_specs=[VM] * len(out),
            scratch_shapes=[pltpu.VMEM((frame + 1, probes, block), f32)],
            name="spread_turn" if turn else "spread",
            **params(2 * slots * rows * probes * block * block, k.size * 2),
        )(flag, ids, x, k)

    return call


def fill_frame(frame_ref, odd, own, even, crossed):
    rows = own.shape[0]
    frame_ref[pl.ds(REACH, rows)] = own[...]
    frame_ref[pl.ds((1 - odd) * (REACH + rows), REACH)] = even[...]
    frame_ref[pl.ds(odd * (REACH + rows), REACH)] = crossed[...]
    frame_ref[rows + 2 * REACH] = jnp.zeros(own.shape[1:], own.dtype)


def direct(flag, ids, x, even, crossed, kt, own, onsite):
    slots, rows, block, _ = kt.shape
    probes = x.shape[1]

    def kernel(flag_ref, ids_ref, x_ref, e_ref, o_ref, kt_ref, own_ref, site_ref, out_ref, frame):
        fill_frame(frame, flag_ref[1], x_ref, e_ref, o_ref)

        def body(count):
            for c in range(rows):
                acc = own_ref[c] + site_ref[pl.ds(c, 1)] * x_ref[c].astype(f32)
                for m in range(0, count, 2):
                    pair = [frame[ids_ref[c, m]], frame[ids_ref[c, m + 1]]]
                    weights = jnp.concatenate([kt_ref[m, c], kt_ref[m + 1, c]], axis=0)
                    acc = acc + dot(jnp.concatenate(pair, axis=1), weights, NN)
                out_ref[c] = acc

        by_size(flag_ref, slots, body)

    return pl.pallas_call(
        kernel,
        out_shape=jax.ShapeDtypeStruct((rows, probes, block), f32),
        in_specs=[SM, SM, VM, VM, VM, VM, VM, VM],
        out_specs=VM,
        scratch_shapes=[pltpu.VMEM((rows + 2 * REACH + 1, probes, block), bf16)],
        name="direct",
        **params(2 * slots * rows * probes * block * block, kt.size * 2),
    )(flag, ids, x, even, crossed, kt, own, onsite)


def images(flag, v, w, k):
    slots, rows, block, _ = k.shape
    probes = v.shape[1]

    def kernel(flag_ref, v_ref, w_ref, k_ref, out_ref):
        def body(count):
            for c in range(rows):
                left = jnp.concatenate([w_ref[c], v_ref[c]], axis=0)
                for m in range(0, count, 2):
                    out = dot(left, jnp.concatenate([k_ref[m, c], k_ref[m + 1, c]], axis=1), NN)
                    out_ref[m, c] = out[:, :block]
                    out_ref[m + 1, c] = out[:, block:]

        by_size(flag_ref, slots, body)

    return pl.pallas_call(
        kernel,
        out_shape=jax.ShapeDtypeStruct((slots, rows, 2 * probes, block), f32),
        in_specs=[SM, VM, VM, VM],
        out_specs=VM,
        name="images",
        **params(4 * slots * rows * probes * block * block, k.size * 2),
    )(flag, v, w, k)


def forces(flag, ids, bond, v, v_even, v_crossed, w, w_even, w_crossed, kt, image):
    slots, rows, block, _ = kt.shape
    probes = v.shape[1]
    frame_rows = rows + 2 * REACH
    sub = 8

    def folded(value):
        parts = [value[i : i + sub] for i in range(0, value.shape[0], sub)]
        while len(parts) > 1:
            parts = [a + b for a, b in zip(parts[::2], parts[1::2])]
        return parts[0]

    def kernel(flag_ref, ids_ref, bond_ref, *refs):
        v_ref, ve_ref, vo_ref, w_ref, we_ref, wo_ref, kt_ref, image_ref = refs[:8]
        own_ref, even_ref, odd_ref, vf, wf, acc = refs[8:]
        odd = flag_ref[1]
        fill_frame(vf, odd, v_ref, ve_ref, vo_ref)
        fill_frame(wf, odd, w_ref, we_ref, wo_ref)
        acc[...] = jnp.zeros_like(acc)

        def body(count):
            for c in range(rows):
                mine = jnp.concatenate([w_ref[c], v_ref[c]], axis=0).astype(f32)
                row = [jnp.zeros((sub, block), f32)] * 3
                for m in range(0, count, 2):
                    far = []
                    for slot in (m, m + 1):
                        d = ids_ref[c, slot]
                        far.append(jnp.concatenate([vf[d], wf[d]], axis=0))
                    weights = jnp.concatenate([kt_ref[m, c], kt_ref[m + 1, c]], axis=1)
                    out = dot(jnp.concatenate(far, axis=0), weights, NN)
                    direct_parts = [out[: 2 * probes, :block], out[2 * probes :, block:]]
                    for slot, other, part in zip((m, m + 1), far, direct_parts):
                        d = ids_ref[c, slot]
                        row_part = folded(mine * part)
                        col_part = folded(other.astype(f32) * image_ref[slot, c])
                        for axis in range(3):
                            b = bond_ref[axis * rows + c, slot]
                            row[axis] = row[axis] + b * row_part
                            acc[d, axis] = acc[d, axis] + b * col_part
                for axis in range(3):
                    acc[c + REACH, axis] = acc[c + REACH, axis] - row[axis]

        by_size(flag_ref, slots, body)

        def taken(start, count):
            return DECAY * jnp.sum(acc[pl.ds(start, count)], axis=2)

        own_ref[...] = taken(REACH, rows)
        even_ref[...] = taken((1 - odd) * (REACH + rows), REACH)
        odd_ref[...] = taken(odd * (REACH + rows), REACH)

    side = jax.ShapeDtypeStruct((REACH, 3, block), f32)
    frame = pltpu.VMEM((frame_rows + 1, probes, block), bf16)
    return pl.pallas_call(
        kernel,
        out_shape=[jax.ShapeDtypeStruct((rows, 3, block), f32), side, side],
        in_specs=[SM, SM, SM] + [VM] * 8,
        out_specs=[VM] * 3,
        scratch_shapes=[frame, frame, pltpu.VMEM((frame_rows + 1, 3, sub, block), f32)],
        name="forces",
        **params(4 * slots * rows * probes * block * block, kt.size * 2 + image.size * 4),
    )(flag, ids, bond, v, v_even, v_crossed, w, w_even, w_crossed, kt, image)


def local(probes, onsite, hopping, block_col, atom_of, bond_dir, chemical_potential):
    rows, _, block = probes.shape
    orbitals = float(rows * lax.axis_size("clus") * block)
    flag, ids, bond, coeffs = prepared(
        block_col.T, jnp.transpose(bond_dir, (0, 2, 1)), chemical_potential
    )
    x = probes
    even, crossed = exchange(x, x)
    v_even, v_crossed = even, crossed
    cheb = [probes]
    for term in range(1, ORDER + 1):
        outs = spread(flag, ids, x, hopping)(term == 1)
        if term == 1:
            turned = outs[3]
        back_even, back_crossed = exchange(outs[1], outs[2])
        image = direct(flag, ids, x, even, crossed, turned, outs[0], onsite)
        if term == ORDER:
            break
        image = image + (back_even.astype(f32) + back_crossed.astype(f32))
        cheb.append(image if term == 1 else 2.0 * image - cheb[-2].astype(f32))
        x = cheb[-1].astype(bf16)
        even, crossed = exchange(x, x)
        if term == 2:
            sums = doubled_sum(moments(coeffs, *cheb), "clus")
    weighted, head = closed(coeffs, sums, orbitals, cheb, image, back_even, back_crossed)
    w_even, w_crossed = exchange(weighted, weighted)
    image = images(flag, probes, weighted, hopping)
    own, to_even, to_odd = forces(
        flag, ids, bond, probes, v_even, v_crossed, weighted, w_even, w_crossed, turned, image
    )
    from_even, from_odd = exchange(to_even, to_odd)
    part = packed(head, own, from_even, from_odd, atom_of)
    count = lax.axis_size("probe")
    parts = [part]
    step = 1
    while step < count:
        part = sum(parts[1:], parts[0])
        parts = [part, lax.ppermute(part, "probe", [(i, i ^ step) for i in range(count)])]
        step *= 2
    return tuple(unpacked(parts, rows, orbitals))


def solution(mesh):
    placed = (
        P("clus", "probe", None),
        P("clus", None),
        P(None, "clus", None, None),
        P(None, "clus"),
        P("clus", None),
        P(None, None, "clus"),
        P(),
    )
    return jax.shard_map(
        local,
        mesh=mesh,
        in_specs=placed,
        out_specs=(P("clus", None), P(), P(None, "clus")),
        check_vma=False,
    )
```

```python
import functools

import jax
import jax.numpy as jnp
import numpy as np
from jax import lax
from jax.experimental import pallas as pl
from jax.experimental.pallas import tpu as pltpu
from jax.sharding import PartitionSpec as P


ATOMS = 32
REACH = 12
PROBE_VECTORS = 128
ORDER = 4
DECAY = 50.0
SMEARING_TEMP = 0.1
QUAD_NODES = 64
HALF_SLOTS = 10

bf16 = jnp.bfloat16
f32 = jnp.float32
NN = (((1,), (0,)), ((), ()))
NT = (((1,), (1,)), ((), ()))
dot = functools.partial(lax.dot_general, preferred_element_type=f32)
VM = pl.BlockSpec(memory_space=pltpu.VMEM)
SM = pl.BlockSpec(memory_space=pltpu.SMEM)


def params(flops, nbytes):
    return dict(
        compiler_params=pltpu.CompilerParams(vmem_limit_bytes=8 << 20),
        cost_estimate=pl.CostEstimate(flops=flops, bytes_accessed=nbytes, transcendentals=0),
    )


def quadrature():
    angles = np.pi * (np.arange(QUAD_NODES) + 0.5) / QUAD_NODES
    table = np.zeros((8, 128), np.float32)
    for order in range(ORDER + 1):
        weight = 2.0 / QUAD_NODES * (0.5 if order == 0 else 1.0)
        table[order, :QUAD_NODES] = weight * np.cos(order * angles)
    table[7, :QUAD_NODES] = np.cos(angles)
    return jnp.asarray(table)


def opening(columns, x, k, bond_dir, chemical_potential):
    rows, slots = columns.shape
    probes, block = x.shape[1:]
    frame = rows + 2 * REACH
    halves = (0, HALF_SLOTS, slots)

    def kernel(col_hbm, x_hbm, k_hbm, bond_hbm, table_hbm, mu_ref, *refs):
        flag_ref, ids_ref, out_ref, coeff_ref, own_ref, even_ref, odd_ref, kv_ref, kt_ref = refs[:9]
        acc, col_sm, col_vm, xv, bond_vm, table_vm, sems, small = refs[9:]
        me = lax.axis_index("clus")

        def load(c, half):
            part = pl.ds(halves[half], halves[half + 1] - halves[half])
            return pltpu.make_async_copy(
                k_hbm.at[part, c], kv_ref.at[part, c], sems.at[half, c]
            )

        pairs = ((col_hbm, col_vm), (col_hbm, col_sm), (x_hbm, xv), (table_hbm, table_vm), (bond_hbm, bond_vm))
        copies = [pltpu.make_async_copy(a, b, small.at[i]) for i, (a, b) in enumerate(pairs)]
        for copy in copies:
            copy.start()
        for c in range(rows):
            load(c, 0).start()
        acc[...] = jnp.zeros_like(acc)
        copies[0].wait()
        col = col_vm[...]
        late = lax.broadcasted_iota(jnp.int32, col.shape, 1) >= HALF_SLOTS
        many = jnp.max(jnp.where(late, col, -1)) >= 0
        flag_ref[0] = many.astype(jnp.int32)
        odd = lax.rem(me, 2)
        flag_ref[1] = odd

        @pl.when(many)
        def _():
            for c in range(rows):
                load(c, 1).start()

        ids_ref[...] = jnp.where(col >= 0, col - me * rows + REACH, frame)
        for copy in copies[1:]:
            copy.wait()
        for axis in range(3):
            out_ref[axis * rows : (axis + 1) * rows] = bond_vm[axis].astype(f32)
        energy = (table_vm[7:8] - mu_ref[0]) / SMEARING_TEMP
        occupied = 1.0 / (1.0 + jnp.exp(energy))
        total = jnp.sum(table_vm[...] * occupied, axis=1, keepdims=True)
        coeff_ref[...] = jnp.broadcast_to(total, coeff_ref.shape)

        def body(last):
            for half in range(last):
                for c in range(rows):
                    load(c, half).wait()
                    xc = xv[c]
                    for first in range(halves[half], halves[half + 1], 4):
                        parts, targets = [], []
                        for m in range(first, min(first + 4, halves[half + 1]), 2):
                            pair = [kv_ref[m, c], kv_ref[m + 1, c]]
                            out = dot(xc, jnp.concatenate(pair, axis=1), NN)
                            parts += [out[:, :block], out[:, block:]]
                            for slot in (m, m + 1):
                                at = col_sm[c, slot]
                                targets.append(jnp.where(at >= 0, at - me * rows + REACH, frame))
                            kt_ref[m, c] = pair[0].T
                            kt_ref[m + 1, c] = pair[1].T
                        values = [acc[t] + part for t, part in zip(targets, parts)]
                        for t, value in zip(targets, values):
                            acc[t] = value

        @pl.when(many)
        def _():
            body(2)

        @pl.when(jnp.logical_not(many))
        def _():
            body(1)

        own_ref[...] = acc[pl.ds(REACH, rows)]
        even_ref[...] = acc[pl.ds((1 - odd) * (REACH + rows), REACH)].astype(bf16)
        odd_ref[...] = acc[pl.ds(odd * (REACH + rows), REACH)].astype(bf16)

    side = jax.ShapeDtypeStruct((REACH, probes, block), bf16)
    blocks = jax.ShapeDtypeStruct(k.shape, k.dtype)
    hbm = pl.BlockSpec(memory_space=pltpu.HBM)
    return pl.pallas_call(
        kernel,
        out_shape=[
            jax.ShapeDtypeStruct((2,), jnp.int32),
            jax.ShapeDtypeStruct((rows, slots), jnp.int32),
            jax.ShapeDtypeStruct((3 * rows, slots), f32),
            jax.ShapeDtypeStruct((8, 128), f32),
            jax.ShapeDtypeStruct((rows, probes, block), f32),
            side,
            side,
            blocks,
            blocks,
        ],
        in_specs=[hbm] * 5 + [SM],
        out_specs=[SM] + [VM] * 8,
        scratch_shapes=[
            pltpu.VMEM((frame + 1, probes, block), f32),
            pltpu.SMEM((rows, slots), jnp.int32),
            pltpu.VMEM((rows, slots), jnp.int32),
            pltpu.VMEM(x.shape, x.dtype),
            pltpu.VMEM(bond_dir.shape, bond_dir.dtype),
            pltpu.VMEM((8, 128), f32),
            pltpu.SemaphoreType.DMA((2, rows)),
            pltpu.SemaphoreType.DMA((5,)),
        ],
        name="opening",
        **params(2 * slots * rows * probes * block * block, k.size * 2),
    )(*(pltpu.with_memory_space_constraint(a, pltpu.HBM) for a in (columns, x, k, bond_dir, quadrature())), chemical_potential)


def moments(coeffs, v, first, second):
    _, probes, block = v.shape

    def kernel(coeff_ref, v_ref, a_ref, b_ref, out_ref):
        wide = v_ref[...].astype(f32)
        a, b = a_ref[...], b_ref[...]
        pairs = (wide * wide, wide * a, wide * b, a * b, b * b)
        m0, m1, m2, ab, bb = [jnp.sum(pair, axis=0) for pair in pairs]
        c = [coeff_ref[k : k + 1] for k in range(ORDER + 1)]
        out_ref[0] = m0
        out_ref[1] = (
            c[0] * m0 + c[1] * m1 + c[2] * m2 + c[3] * (2.0 * ab - m1) + c[4] * (2.0 * bb - m0)
        )

    return pl.pallas_call(
        kernel,
        out_shape=jax.ShapeDtypeStruct((2, probes, block), f32),
        in_specs=[VM] * 4,
        out_specs=VM,
        name="moments",
        **params(10 * v.size, 10 * v.size),
    )(coeffs, v, first, second)


def closed(coeffs, sums, orbitals, cheb, image, back_even, back_crossed):
    rows, probes, block = image.shape

    def kernel(coeff_ref, sum_ref, c0, c1, c2, c3, y_ref, e_ref, o_ref, w_ref, head_ref):
        square = jnp.sum(sum_ref[0], axis=1, keepdims=True)
        scale = orbitals / (square * PROBE_VECTORS)
        head_ref[...] = jnp.zeros_like(head_ref)
        head_ref[rows : rows + 1] = jnp.sum(scale * sum_ref[1], axis=0, keepdims=True)
        scale = jnp.broadcast_to(scale, (probes, block))
        c = [coeff_ref[k : k + 1] for k in range(ORDER + 1)]
        for r in range(rows):
            y = y_ref[r] + (e_ref[r].astype(f32) + o_ref[r].astype(f32))
            wide = c0[r].astype(f32)
            fermi = c[0] * wide + c[1] * c1[r]
            fermi = fermi + c[2] * c2[r]
            fermi = fermi + c[3] * c3[r]
            fermi = fermi + c[4] * (2.0 * y - c2[r])
            scaled = fermi * scale
            w_ref[r] = scaled.astype(bf16)
            head_ref[r : r + 1] = jnp.sum(wide * scaled, axis=0, keepdims=True)

    return pl.pallas_call(
        kernel,
        out_shape=[
            jax.ShapeDtypeStruct((rows, probes, block), bf16),
            jax.ShapeDtypeStruct((16, block), f32),
        ],
        in_specs=[VM] * 9,
        out_specs=[VM] * 2,
        name="closed",
        **params(20 * image.size, 30 * image.size),
    )(coeffs, sums, *cheb, image, back_even, back_crossed)


def packed(head, own, from_even, from_odd, atom_of):
    rows, _, block = own.shape
    group = block // ATOMS
    lines = rows // group

    def kernel(head_ref, own_ref, e_ref, o_ref, atom_ref, out_ref):
        out_ref[...] = jnp.zeros_like(out_ref)
        out_ref[: rows + 1] = head_ref[: rows + 1]
        lane = lax.broadcasted_iota(jnp.int32, (block, block), 0)
        for line in range(lines):
            total = jnp.zeros((16, block), f32)
            for part in range(group):
                r = line * group + part
                g = own_ref[r] + e_ref[r] + o_ref[r]
                high = g.astype(bf16)
                rest = g - high.astype(f32)
                middle = rest.astype(bf16)
                low = (rest - middle.astype(f32)).astype(bf16)
                pad = jnp.zeros((16 - 9, block), bf16)
                left = jnp.concatenate([high, middle, low, pad], axis=0)
                hot = (lane == atom_ref[r : r + 1] + part * ATOMS).astype(f32).astype(bf16)
                total = total + dot(left, hot, NT)
            value = total[0:3] + (total[3:6] + total[6:9])
            for axis in range(3):
                at = rows + 1 + axis * lines + line
                out_ref[at : at + 1] = value[axis : axis + 1]

    height = -(-(rows + 1 + 3 * lines) // 8) * 8
    return pl.pallas_call(
        kernel,
        out_shape=jax.ShapeDtypeStruct((height, block), f32),
        in_specs=[VM] * 5,
        out_specs=VM,
        name="packed",
        **params(2 * rows * 16 * block * block, 100000),
    )(head, own, from_even, from_odd, atom_of)


def unpacked(parts, rows, orbitals):
    _, block = parts[0].shape
    lines = rows * ATOMS // block

    def kernel(*refs):
        ins, (density_ref, filling_ref, force_ref) = refs[: len(parts)], refs[len(parts) :]
        total = ins[0][...]
        for other in ins[1:]:
            total = total + other[...]
        density_ref[...] = total[:rows]
        filling_ref[0] = jnp.sum(total[rows : rows + 1]) / orbitals
        for axis in range(3):
            for line in range(lines):
                at = rows + 1 + axis * lines + line
                force_ref[axis : axis + 1, line * block : (line + 1) * block] = total[at : at + 1]

    return pl.pallas_call(
        kernel,
        out_shape=[
            jax.ShapeDtypeStruct((rows, block), f32),
            jax.ShapeDtypeStruct((1,), f32),
            jax.ShapeDtypeStruct((3, lines * block), f32),
        ],
        in_specs=[VM] * len(parts),
        out_specs=[VM, SM, VM],
        name="unpacked",
        **params(10000, 100000),
    )(*parts)


def exchange(even_side, odd_side):
    count = lax.axis_size("clus")
    paired = [(i, i ^ 1) for i in range(count)]
    shifted = [(i, (i + 1 if i % 2 else i - 1) % count) for i in range(count)]
    crossed = lax.ppermute(odd_side, "clus", shifted)
    even = lax.ppermute(even_side, "clus", paired)
    return even, crossed


def doubled(index, part, axis):
    count = lax.axis_size(axis)
    other = lax.ppermute(part, axis, [(i, i ^ (1 << index)) for i in range(count)])
    return part + other


def by_size(flag, slots, body):
    @pl.when(flag[0] != 0)
    def _():
        body(slots)

    @pl.when(flag[0] == 0)
    def _():
        body(HALF_SLOTS)


def spread(flag, ids, x, k):
    slots, rows, block, _ = k.shape
    probes = x.shape[1]
    frame = rows + 2 * REACH

    def kernel(flag_ref, ids_ref, x_ref, k_ref, own_ref, even_ref, odd_ref, acc):
        acc[...] = jnp.zeros_like(acc)

        def body(count):
            for c in range(rows):
                xc = x_ref[c]
                for first in range(0, count, 4):
                    parts, targets = [], []
                    for m in range(first, min(first + 4, count), 2):
                        pair = [k_ref[m, c], k_ref[m + 1, c]]
                        out = dot(xc, jnp.concatenate(pair, axis=1), NN)
                        parts += [out[:, :block], out[:, block:]]
                        targets += [ids_ref[c, m], ids_ref[c, m + 1]]
                    values = [acc[t] + part for t, part in zip(targets, parts)]
                    for t, value in zip(targets, values):
                        acc[t] = value

        by_size(flag_ref, slots, body)
        odd = flag_ref[1]
        own_ref[...] = acc[pl.ds(REACH, rows)]
        even_ref[...] = acc[pl.ds((1 - odd) * (REACH + rows), REACH)].astype(bf16)
        odd_ref[...] = acc[pl.ds(odd * (REACH + rows), REACH)].astype(bf16)

    side = jax.ShapeDtypeStruct((REACH, probes, block), bf16)
    return pl.pallas_call(
        kernel,
        out_shape=[jax.ShapeDtypeStruct((rows, probes, block), f32), side, side],
        in_specs=[SM, SM, VM, VM],
        out_specs=[VM] * 3,
        scratch_shapes=[pltpu.VMEM((frame + 1, probes, block), f32)],
        name="spread",
        **params(2 * slots * rows * probes * block * block, k.size * 2),
    )(flag, ids, x, k)


def fill_frame(frame_ref, odd, own, even, crossed):
    rows = own.shape[0]
    frame_ref[pl.ds(REACH, rows)] = own[...]
    frame_ref[pl.ds((1 - odd) * (REACH + rows), REACH)] = even[...]
    frame_ref[pl.ds(odd * (REACH + rows), REACH)] = crossed[...]
    frame_ref[rows + 2 * REACH] = jnp.zeros(own.shape[1:], own.dtype)


def direct(flag, ids, x, even, crossed, kt, own, onsite):
    slots, rows, block, _ = kt.shape
    probes = x.shape[1]

    def kernel(flag_ref, ids_ref, x_ref, e_ref, o_ref, kt_ref, own_ref, site_ref, out_ref, frame):
        fill_frame(frame, flag_ref[1], x_ref, e_ref, o_ref)

        def body(count):
            for c in range(rows):
                acc = own_ref[c] + site_ref[pl.ds(c, 1)] * x_ref[c].astype(f32)
                for m in range(0, count, 2):
                    pair = [frame[ids_ref[c, m]], frame[ids_ref[c, m + 1]]]
                    weights = jnp.concatenate([kt_ref[m, c], kt_ref[m + 1, c]], axis=0)
                    acc = acc + dot(jnp.concatenate(pair, axis=1), weights, NN)
                out_ref[c] = acc

        by_size(flag_ref, slots, body)

    return pl.pallas_call(
        kernel,
        out_shape=jax.ShapeDtypeStruct((rows, probes, block), f32),
        in_specs=[SM, SM, VM, VM, VM, VM, VM, VM],
        out_specs=VM,
        scratch_shapes=[pltpu.VMEM((rows + 2 * REACH + 1, probes, block), bf16)],
        name="direct",
        **params(2 * slots * rows * probes * block * block, kt.size * 2),
    )(flag, ids, x, even, crossed, kt, own, onsite)


def folded(value):
    parts = [value[i : i + 8] for i in range(0, value.shape[0], 8)]
    while len(parts) > 1:
        parts = [a + b for a, b in zip(parts[::2], parts[1::2])]
    return parts[0]


def near_forces(flag, ids, bond, v, v_even, v_crossed, w, k, kt):
    slots, rows, block, _ = kt.shape
    probes = v.shape[1]
    frame = rows + 2 * REACH

    def kernel(flag_ref, ids_ref, bond_ref, *refs):
        v_ref, ve_ref, vo_ref, w_ref, k_ref, kt_ref, acc, image_ref, vf = refs
        fill_frame(vf, flag_ref[1], v_ref, ve_ref, vo_ref)
        acc[...] = jnp.zeros_like(acc)

        def body(count):
            for c in range(rows):
                mine = w_ref[c].astype(f32)
                left = jnp.concatenate([w_ref[c], v_ref[c]], axis=0)
                row = [jnp.zeros((8, block), f32)] * 3
                for m in range(0, count, 2):
                    two = (m, m + 1)
                    far = [vf[ids_ref[c, slot]] for slot in two]
                    out = dot(left, jnp.concatenate([k_ref[slot, c] for slot in two], axis=1), NN)
                    weights = jnp.concatenate([kt_ref[slot, c] for slot in two], axis=1)
                    back = dot(jnp.concatenate(far, axis=0), weights, NN)
                    for i, slot in enumerate(two):
                        d = ids_ref[c, slot]
                        lanes = slice(i * block, (i + 1) * block)
                        image_ref[slot, c] = out[probes:, lanes]
                        col_part = folded(far[i].astype(f32) * out[:probes, lanes])
                        row_part = folded(mine * back[i * probes : (i + 1) * probes, lanes])
                        for axis in range(3):
                            b = bond_ref[axis * rows + c, slot]
                            row[axis] = row[axis] + b * row_part
                            acc[d, axis] = acc[d, axis] + b * col_part
                for axis in range(3):
                    acc[c + REACH, axis] = acc[c + REACH, axis] - row[axis]

        by_size(flag_ref, slots, body)

    return pl.pallas_call(
        kernel,
        out_shape=[
            jax.ShapeDtypeStruct((frame + 1, 3, 8, block), f32),
            jax.ShapeDtypeStruct((slots, rows, probes, block), f32),
        ],
        in_specs=[SM, SM, SM] + [VM] * 6,
        out_specs=[VM] * 2,
        scratch_shapes=[pltpu.VMEM((frame + 1, probes, block), bf16)],
        name="near_forces",
        **params(6 * slots * rows * probes * block * block, k.size * 4),
    )(flag, ids, bond, v, v_even, v_crossed, w, k, kt)


def far_forces(flag, ids, bond, v, w, w_even, w_crossed, kt, image, started):
    slots, rows, block, _ = kt.shape
    probes = v.shape[1]
    frame = rows + 2 * REACH

    def kernel(flag_ref, ids_ref, bond_ref, *refs):
        v_ref, w_ref, we_ref, wo_ref, kt_ref, image_ref, start_ref = refs[:7]
        own_ref, even_ref, odd_ref, wf, acc = refs[7:]
        odd = flag_ref[1]
        fill_frame(wf, odd, w_ref, we_ref, wo_ref)
        acc[...] = start_ref[...]

        def body(count):
            for c in range(rows):
                mine = v_ref[c].astype(f32)
                row = [jnp.zeros((8, block), f32)] * 3
                for m in range(0, count, 2):
                    two = (m, m + 1)
                    far = [wf[ids_ref[c, slot]] for slot in two]
                    weights = jnp.concatenate([kt_ref[slot, c] for slot in two], axis=1)
                    back = dot(jnp.concatenate(far, axis=0), weights, NN)
                    for i, slot in enumerate(two):
                        d = ids_ref[c, slot]
                        lanes = slice(i * block, (i + 1) * block)
                        col_part = folded(far[i].astype(f32) * image_ref[slot, c])
                        row_part = folded(mine * back[i * probes : (i + 1) * probes, lanes])
                        for axis in range(3):
                            b = bond_ref[axis * rows + c, slot]
                            row[axis] = row[axis] + b * row_part
                            acc[d, axis] = acc[d, axis] + b * col_part
                for axis in range(3):
                    acc[c + REACH, axis] = acc[c + REACH, axis] - row[axis]

        by_size(flag_ref, slots, body)

        def taken(start, count):
            return DECAY * jnp.sum(acc[pl.ds(start, count)], axis=2)

        own_ref[...] = taken(REACH, rows)
        even_ref[...] = taken((1 - odd) * (REACH + rows), REACH)
        odd_ref[...] = taken(odd * (REACH + rows), REACH)

    side = jax.ShapeDtypeStruct((REACH, 3, block), f32)
    return pl.pallas_call(
        kernel,
        out_shape=[jax.ShapeDtypeStruct((rows, 3, block), f32), side, side],
        in_specs=[SM, SM, SM] + [VM] * 7,
        out_specs=[VM] * 3,
        scratch_shapes=[
            pltpu.VMEM((frame + 1, probes, block), bf16),
            pltpu.VMEM((frame + 1, 3, 8, block), f32),
        ],
        name="far_forces",
        **params(2 * slots * rows * probes * block * block, kt.size * 2 + image.size * 4),
    )(flag, ids, bond, v, w, w_even, w_crossed, kt, image, started)


def local(probes, onsite, hopping, block_col, atom_of, bond_dir, chemical_potential):
    rows, _, block = probes.shape
    orbitals = float(rows * lax.axis_size("clus") * block)
    x = probes
    even, crossed = exchange(x, x)
    v_even, v_crossed = even, crossed
    flag, ids, bond, coeffs, *outs, k, kt = opening(
        block_col.T, x, hopping, jnp.transpose(bond_dir, (0, 2, 1)), chemical_potential
    )
    rounds = (lax.axis_size("clus") - 1).bit_length()
    cheb = [probes]
    for term in range(1, ORDER + 1):
        if term == 3:
            sums = doubled(0, moments(coeffs, *cheb), "clus")
        if term > 1:
            outs = spread(flag, ids, x, k)
        own, to_even, to_odd = outs
        back_even, back_crossed = exchange(to_even, to_odd)
        if term > 2:
            sums = doubled(term - 2, sums, "clus")
        image = direct(flag, ids, x, even, crossed, kt, own, onsite)
        if term == ORDER:
            break
        image = image + (back_even.astype(f32) + back_crossed.astype(f32))
        cheb.append(image if term == 1 else 2.0 * image - cheb[-2].astype(f32))
        x = cheb[-1].astype(bf16)
        even, crossed = exchange(x, x)
    for index in range(3, rounds):
        sums = doubled(index, sums, "clus")
    weighted, head = closed(coeffs, sums, orbitals, cheb, image, back_even, back_crossed)
    w_even, w_crossed = exchange(weighted, weighted)
    started, image = near_forces(flag, ids, bond, probes, v_even, v_crossed, weighted, k, kt)
    own, to_even, to_odd = far_forces(
        flag, ids, bond, probes, weighted, w_even, w_crossed, kt, image, started
    )
    from_even, from_odd = exchange(to_even, to_odd)
    part = packed(head, own, from_even, from_odd, atom_of)
    count = lax.axis_size("probe")
    parts = [part]
    step = 1
    while step < count:
        part = sum(parts[1:], parts[0])
        parts = [part, lax.ppermute(part, "probe", [(i, i ^ step) for i in range(count)])]
        step *= 2
    return tuple(unpacked(parts, rows, orbitals))


def solution(mesh):
    placed = (
        P("clus", "probe", None),
        P("clus", None),
        P(None, "clus", None, None),
        P(None, "clus"),
        P("clus", None),
        P(None, None, "clus"),
        P(),
    )
    return jax.shard_map(
        local,
        mesh=mesh,
        in_specs=placed,
        out_specs=(P("clus", None), P(), P(None, "clus")),
        check_vma=False,
    )
```

```python
import functools

import jax
import jax.numpy as jnp
import numpy as np
from jax import lax
from jax.experimental import pallas as pl
from jax.experimental.pallas import tpu as pltpu
from jax.sharding import PartitionSpec as P


ATOMS = 32
REACH = 12
PROBE_VECTORS = 128
ORDER = 4
DECAY = 50.0
SMEARING_TEMP = 0.1
QUAD_NODES = 64
HALF_SLOTS = 10
CHUNKS = 3
AHEAD = 6

bf16 = jnp.bfloat16
f32 = jnp.float32
NN = (((1,), (0,)), ((), ()))
NT = (((1,), (1,)), ((), ()))
dot = functools.partial(lax.dot_general, preferred_element_type=f32)
VM = pl.BlockSpec(memory_space=pltpu.VMEM)
SM = pl.BlockSpec(memory_space=pltpu.SMEM)


def params(flops, nbytes):
    return dict(
        compiler_params=pltpu.CompilerParams(vmem_limit_bytes=8 << 20),
        cost_estimate=pl.CostEstimate(flops=flops, bytes_accessed=nbytes, transcendentals=0),
    )


def quadrature():
    angles = np.pi * (np.arange(QUAD_NODES) + 0.5) / QUAD_NODES
    table = np.zeros((8, 128), np.float32)
    for order in range(ORDER + 1):
        weight = 2.0 / QUAD_NODES * (0.5 if order == 0 else 1.0)
        table[order, :QUAD_NODES] = weight * np.cos(order * angles)
    table[7, :QUAD_NODES] = np.cos(angles)
    return jnp.asarray(table)


def opening(columns, x, k, bond_dir, chemical_potential):
    rows, slots = columns.shape
    probes, block = x.shape[1:]
    frame = rows + 2 * REACH
    halves = (0, HALF_SLOTS, slots)
    height = rows // CHUNKS

    def kernel(col_hbm, x_hbm, k_hbm, bond_hbm, table_hbm, mu_ref, *refs):
        flag_ref, ids_ref, at_ref, out_ref, coeff_ref, own_ref, even_ref, odd_ref, kv_ref, kt_ref = refs[:10]
        acc, col_sm, col_vm, xv, bond_vm, table_vm, sems, small = refs[10:]
        me = lax.axis_index("clus")

        def load(index):
            half, chunk = divmod(index, CHUNKS)
            part = pl.ds(halves[half], halves[half + 1] - halves[half])
            group = pl.ds(chunk * height, height)
            return pltpu.make_async_copy(
                k_hbm.at[part, group], kv_ref.at[part, group], sems.at[index]
            )

        pairs = (
            (col_hbm, col_vm),
            (col_hbm, col_sm),
            (x_hbm, xv),
            (table_hbm, table_vm),
            (bond_hbm, bond_vm),
        )
        copies = [pltpu.make_async_copy(a, b, small.at[i]) for i, (a, b) in enumerate(pairs)]
        for copy in copies:
            copy.start()
        for index in range(min(AHEAD, CHUNKS)):
            load(index).start()
        acc[...] = jnp.zeros_like(acc)
        copies[0].wait()
        col = col_vm[...]
        late = lax.broadcasted_iota(jnp.int32, col.shape, 1) >= HALF_SLOTS
        many = jnp.max(jnp.where(late, col, -1)) >= 0
        flag_ref[0] = many.astype(jnp.int32)
        odd = lax.rem(me, 2)
        flag_ref[1] = odd

        ids = jnp.where(col >= 0, col - me * rows + REACH, frame)
        ids_ref[...] = ids
        side = lax.broadcasted_iota(jnp.int32, (rows, REACH), 1) + odd * (REACH + rows)
        at = jnp.full((rows, REACH), slots, jnp.int32)
        for m in range(slots):
            at = jnp.where(ids[:, m : m + 1] == side, m, at)
        at_ref[...] = at
        for c in range(rows):
            kv_ref[slots, c] = jnp.zeros((block, block), kv_ref.dtype)
        for copy in copies[1:]:
            copy.wait()
        for axis in range(3):
            out_ref[axis * rows : (axis + 1) * rows] = bond_vm[axis].astype(f32)
        energy = (table_vm[7:8] - mu_ref[0]) / SMEARING_TEMP
        occupied = 1.0 / (1.0 + jnp.exp(energy))
        total = jnp.sum(table_vm[...] * occupied, axis=1, keepdims=True)
        coeff_ref[...] = jnp.broadcast_to(total, coeff_ref.shape)

        def body(last):
            for index in range(last * CHUNKS):
                half, chunk = divmod(index, CHUNKS)
                if index == 0:
                    for later in range(min(AHEAD, CHUNKS), min(AHEAD, last * CHUNKS)):
                        load(later).start()
                load(index).wait()
                if index + AHEAD < last * CHUNKS:
                    load(index + AHEAD).start()
                for c in range(chunk * height, (chunk + 1) * height):
                    xc = xv[c]
                    for first in range(halves[half], halves[half + 1], 4):
                        parts, targets = [], []
                        for m in range(first, min(first + 4, halves[half + 1]), 2):
                            pair = [kv_ref[m, c], kv_ref[m + 1, c]]
                            out = dot(xc, jnp.concatenate(pair, axis=1), NN)
                            parts += [out[:, :block], out[:, block:]]
                            for slot in (m, m + 1):
                                at = col_sm[c, slot]
                                targets.append(jnp.where(at >= 0, at - me * rows + REACH, frame))
                            kt_ref[m, c] = pair[0].T
                            kt_ref[m + 1, c] = pair[1].T
                        values = [acc[t] + part for t, part in zip(targets, parts)]
                        for t, value in zip(targets, values):
                            acc[t] = value

        @pl.when(many)
        def _():
            body(2)

        @pl.when(jnp.logical_not(many))
        def _():
            body(1)

        own_ref[...] = acc[pl.ds(REACH, rows)]
        even_ref[...] = acc[pl.ds((1 - odd) * (REACH + rows), REACH)].astype(bf16)
        odd_ref[...] = acc[pl.ds(odd * (REACH + rows), REACH)].astype(bf16)

    side = jax.ShapeDtypeStruct((REACH, probes, block), bf16)
    hbm = pl.BlockSpec(memory_space=pltpu.HBM)
    operands = (columns, x, k, bond_dir, quadrature())
    return pl.pallas_call(
        kernel,
        out_shape=[
            jax.ShapeDtypeStruct((2,), jnp.int32),
            jax.ShapeDtypeStruct((rows, slots), jnp.int32),
            jax.ShapeDtypeStruct((rows, REACH), jnp.int32),
            jax.ShapeDtypeStruct((3 * rows, slots), f32),
            jax.ShapeDtypeStruct((8, 128), f32),
            jax.ShapeDtypeStruct((rows, probes, block), f32),
            side,
            side,
            jax.ShapeDtypeStruct((slots + 1, *k.shape[1:]), k.dtype),
            jax.ShapeDtypeStruct(k.shape, k.dtype),
        ],
        in_specs=[hbm] * 5 + [SM],
        out_specs=[SM] + [VM] * 9,
        scratch_shapes=[
            pltpu.VMEM((frame + 1, probes, block), f32),
            pltpu.SMEM((rows, slots), jnp.int32),
            pltpu.VMEM((rows, slots), jnp.int32),
            pltpu.VMEM(x.shape, x.dtype),
            pltpu.VMEM(bond_dir.shape, bond_dir.dtype),
            pltpu.VMEM((8, 128), f32),
            pltpu.SemaphoreType.DMA((2 * CHUNKS,)),
            pltpu.SemaphoreType.DMA((5,)),
        ],
        name="opening",
        **params(2 * slots * rows * probes * block * block, k.size * 2),
    )(*(pltpu.with_memory_space_constraint(a, pltpu.HBM) for a in operands), chemical_potential)


def moments(coeffs, v, first, second):
    _, probes, block = v.shape

    def kernel(coeff_ref, v_ref, a_ref, b_ref, out_ref):
        wide = v_ref[...].astype(f32)
        a, b = a_ref[...], b_ref[...]
        pairs = (wide * wide, wide * a, wide * b, a * b, b * b)
        m0, m1, m2, ab, bb = [jnp.sum(pair, axis=0) for pair in pairs]
        c = [coeff_ref[k : k + 1] for k in range(ORDER + 1)]
        out_ref[0] = m0
        out_ref[1] = (
            c[0] * m0 + c[1] * m1 + c[2] * m2 + c[3] * (2.0 * ab - m1) + c[4] * (2.0 * bb - m0)
        )

    return pl.pallas_call(
        kernel,
        out_shape=jax.ShapeDtypeStruct((2, probes, block), f32),
        in_specs=[VM] * 4,
        out_specs=VM,
        name="moments",
        **params(10 * v.size, 10 * v.size),
    )(coeffs, v, first, second)


def closed(coeffs, sums, orbitals, cheb, image, back_even, back_crossed):
    rows, probes, block = image.shape

    def kernel(coeff_ref, sum_ref, c0, c1, c2, c3, y_ref, e_ref, o_ref, w_ref, head_ref):
        square = jnp.sum(sum_ref[0], axis=1, keepdims=True)
        scale = orbitals / (square * PROBE_VECTORS)
        head_ref[...] = jnp.zeros_like(head_ref)
        head_ref[rows : rows + 1] = jnp.sum(scale * sum_ref[1], axis=0, keepdims=True)
        scale = jnp.broadcast_to(scale, (probes, block))
        c = [coeff_ref[k : k + 1] for k in range(ORDER + 1)]
        for r in range(rows):
            y = y_ref[r] + (e_ref[r].astype(f32) + o_ref[r].astype(f32))
            wide = c0[r].astype(f32)
            fermi = c[0] * wide + c[1] * c1[r]
            fermi = fermi + c[2] * c2[r]
            fermi = fermi + c[3] * c3[r]
            fermi = fermi + c[4] * (2.0 * y - c2[r])
            scaled = fermi * scale
            w_ref[r] = scaled.astype(bf16)
            head_ref[r : r + 1] = jnp.sum(wide * scaled, axis=0, keepdims=True)

    return pl.pallas_call(
        kernel,
        out_shape=[
            jax.ShapeDtypeStruct((rows, probes, block), bf16),
            jax.ShapeDtypeStruct((16, block), f32),
        ],
        in_specs=[VM] * 9,
        out_specs=[VM] * 2,
        name="closed",
        **params(20 * image.size, 30 * image.size),
    )(coeffs, sums, *cheb, image, back_even, back_crossed)


def packed(head, own, from_even, from_odd, atom_of):
    rows, _, block = own.shape
    group = block // ATOMS
    lines = rows // group

    def kernel(head_ref, own_ref, e_ref, o_ref, atom_ref, out_ref):
        out_ref[...] = jnp.zeros_like(out_ref)
        out_ref[: rows + 1] = head_ref[: rows + 1]
        lane = lax.broadcasted_iota(jnp.int32, (block, block), 0)
        for line in range(lines):
            total = jnp.zeros((16, block), f32)
            for part in range(group):
                r = line * group + part
                g = own_ref[r] + e_ref[r] + o_ref[r]
                high = g.astype(bf16)
                rest = g - high.astype(f32)
                middle = rest.astype(bf16)
                low = (rest - middle.astype(f32)).astype(bf16)
                pad = jnp.zeros((16 - 9, block), bf16)
                left = jnp.concatenate([high, middle, low, pad], axis=0)
                hot = (lane == atom_ref[r : r + 1] + part * ATOMS).astype(f32).astype(bf16)
                total = total + dot(left, hot, NT)
            value = total[0:3] + (total[3:6] + total[6:9])
            for axis in range(3):
                at = rows + 1 + axis * lines + line
                out_ref[at : at + 1] = value[axis : axis + 1]

    height = -(-(rows + 1 + 3 * lines) // 8) * 8
    return pl.pallas_call(
        kernel,
        out_shape=jax.ShapeDtypeStruct((height, block), f32),
        in_specs=[VM] * 5,
        out_specs=VM,
        name="packed",
        **params(2 * rows * 16 * block * block, 100000),
    )(head, own, from_even, from_odd, atom_of)


def unpacked(parts, rows, orbitals):
    _, block = parts[0].shape
    lines = rows * ATOMS // block

    def kernel(*refs):
        ins, (density_ref, filling_ref, force_ref) = refs[: len(parts)], refs[len(parts) :]
        total = ins[0][...]
        for other in ins[1:]:
            total = total + other[...]
        density_ref[...] = total[:rows]
        filling_ref[0] = jnp.sum(total[rows : rows + 1]) / orbitals
        for axis in range(3):
            for line in range(lines):
                at = rows + 1 + axis * lines + line
                force_ref[axis : axis + 1, line * block : (line + 1) * block] = total[at : at + 1]

    return pl.pallas_call(
        kernel,
        out_shape=[
            jax.ShapeDtypeStruct((rows, block), f32),
            jax.ShapeDtypeStruct((1,), f32),
            jax.ShapeDtypeStruct((3, lines * block), f32),
        ],
        in_specs=[VM] * len(parts),
        out_specs=[VM, SM, VM],
        name="unpacked",
        **params(10000, 100000),
    )(*parts)


def exchange(even_side, odd_side):
    count = lax.axis_size("clus")
    paired = [(i, i ^ 1) for i in range(count)]
    shifted = [(i, (i + 1 if i % 2 else i - 1) % count) for i in range(count)]
    crossed = lax.ppermute(odd_side, "clus", shifted)
    even = lax.ppermute(even_side, "clus", paired)
    return even, crossed


def doubled(index, part, axis):
    count = lax.axis_size(axis)
    other = lax.ppermute(part, axis, [(i, i ^ (1 << index)) for i in range(count)])
    return part + other


def by_size(flag, slots, body):
    @pl.when(flag[0] != 0)
    def _():
        body(slots)

    @pl.when(flag[0] == 0)
    def _():
        body(HALF_SLOTS)


def ahead(flag, at, x, k):
    _, rows, block, _ = k.shape
    probes = x.shape[1]

    def kernel(flag_ref, at_ref, x_ref, k_ref, out_ref):
        def body(above):
            for j in range(REACH):
                reach = list(range(j, rows)) if above else list(range(min(j + 1, rows)))
                acc = None
                for first in range(0, len(reach), 2):
                    group = reach[first : first + 2]
                    left = jnp.concatenate([x_ref[c] for c in group], axis=1)
                    right = jnp.concatenate([k_ref[at_ref[c, j], c] for c in group], axis=0)
                    part = dot(left, right, NN)
                    acc = part if acc is None else acc + part
                out_ref[j] = acc.astype(bf16)

        @pl.when(flag_ref[1] == 0)
        def _():
            body(False)

        @pl.when(flag_ref[1] != 0)
        def _():
            body(True)

    return pl.pallas_call(
        kernel,
        out_shape=jax.ShapeDtypeStruct((REACH, probes, block), bf16),
        in_specs=[SM, SM, VM, VM],
        out_specs=VM,
        name="ahead",
        **params(80 * 2 * probes * block * block, 80 * 2 * block * block),
    )(flag, at, x, k)


def spread(flag, ids, x, k):
    rows, slots = ids.shape
    _, probes, block = x.shape
    frame = rows + 2 * REACH

    def kernel(flag_ref, ids_ref, x_ref, k_ref, own_ref, even_ref, acc):
        acc[...] = jnp.zeros_like(acc)

        def body(count):
            for c in range(rows):
                xc = x_ref[c]
                for first in range(0, count, 4):
                    parts, targets = [], []
                    for m in range(first, min(first + 4, count), 2):
                        pair = [k_ref[m, c], k_ref[m + 1, c]]
                        out = dot(xc, jnp.concatenate(pair, axis=1), NN)
                        parts += [out[:, :block], out[:, block:]]
                        targets += [ids_ref[c, m], ids_ref[c, m + 1]]
                    values = [acc[t] + part for t, part in zip(targets, parts)]
                    for t, value in zip(targets, values):
                        acc[t] = value

        by_size(flag_ref, slots, body)
        odd = flag_ref[1]
        own_ref[...] = acc[pl.ds(REACH, rows)]
        even_ref[...] = acc[pl.ds((1 - odd) * (REACH + rows), REACH)].astype(bf16)

    side = jax.ShapeDtypeStruct((REACH, probes, block), bf16)
    return pl.pallas_call(
        kernel,
        out_shape=[jax.ShapeDtypeStruct((rows, probes, block), f32), side],
        in_specs=[SM, SM, VM, VM],
        out_specs=[VM] * 2,
        scratch_shapes=[pltpu.VMEM((frame + 1, probes, block), f32)],
        name="spread",
        **params(2 * slots * rows * probes * block * block, k.size * 2),
    )(flag, ids, x, k)


def fill_frame(frame_ref, odd, own, even, crossed):
    rows = own.shape[0]
    frame_ref[pl.ds(REACH, rows)] = own[...]
    frame_ref[pl.ds((1 - odd) * (REACH + rows), REACH)] = even[...]
    frame_ref[pl.ds(odd * (REACH + rows), REACH)] = crossed[...]
    frame_ref[rows + 2 * REACH] = jnp.zeros(own.shape[1:], own.dtype)


def direct(flag, ids, x, even, crossed, kt, own, onsite):
    slots, rows, block, _ = kt.shape
    probes = x.shape[1]

    def kernel(flag_ref, ids_ref, x_ref, e_ref, o_ref, kt_ref, own_ref, site_ref, out_ref, frame):
        fill_frame(frame, flag_ref[1], x_ref, e_ref, o_ref)

        def body(count):
            for c in range(rows):
                acc = own_ref[c] + site_ref[pl.ds(c, 1)] * x_ref[c].astype(f32)
                for m in range(0, count, 2):
                    pair = [frame[ids_ref[c, m]], frame[ids_ref[c, m + 1]]]
                    weights = jnp.concatenate([kt_ref[m, c], kt_ref[m + 1, c]], axis=0)
                    acc = acc + dot(jnp.concatenate(pair, axis=1), weights, NN)
                out_ref[c] = acc

        by_size(flag_ref, slots, body)

    return pl.pallas_call(
        kernel,
        out_shape=jax.ShapeDtypeStruct((rows, probes, block), f32),
        in_specs=[SM, SM, VM, VM, VM, VM, VM, VM],
        out_specs=VM,
        scratch_shapes=[pltpu.VMEM((rows + 2 * REACH + 1, probes, block), bf16)],
        name="direct",
        **params(2 * slots * rows * probes * block * block, kt.size * 2),
    )(flag, ids, x, even, crossed, kt, own, onsite)


def folded(value):
    parts = [value[i : i + 8] for i in range(0, value.shape[0], 8)]
    while len(parts) > 1:
        parts = [a + b for a, b in zip(parts[::2], parts[1::2])]
    return parts[0]


def near_forces(flag, ids, bond, v, v_even, v_crossed, w, k, kt):
    slots, rows, block, _ = kt.shape
    probes = v.shape[1]
    frame = rows + 2 * REACH

    def kernel(flag_ref, ids_ref, bond_ref, *refs):
        v_ref, ve_ref, vo_ref, w_ref, k_ref, kt_ref, acc, image_ref, vf = refs
        fill_frame(vf, flag_ref[1], v_ref, ve_ref, vo_ref)
        acc[...] = jnp.zeros_like(acc)

        def body(count):
            for c in range(rows):
                mine = w_ref[c].astype(f32)
                left = jnp.concatenate([w_ref[c], v_ref[c]], axis=0)
                row = [jnp.zeros((8, block), f32)] * 3
                for m in range(0, count, 2):
                    two = (m, m + 1)
                    far = [vf[ids_ref[c, slot]] for slot in two]
                    out = dot(left, jnp.concatenate([k_ref[slot, c] for slot in two], axis=1), NN)
                    weights = jnp.concatenate([kt_ref[slot, c] for slot in two], axis=1)
                    back = dot(jnp.concatenate(far, axis=0), weights, NN)
                    for i, slot in enumerate(two):
                        d = ids_ref[c, slot]
                        lanes = slice(i * block, (i + 1) * block)
                        image_ref[slot, c] = out[probes:, lanes]
                        col_part = folded(far[i].astype(f32) * out[:probes, lanes])
                        row_part = folded(mine * back[i * probes : (i + 1) * probes, lanes])
                        for axis in range(3):
                            b = bond_ref[axis * rows + c, slot]
                            row[axis] = row[axis] + b * row_part
                            acc[d, axis] = acc[d, axis] + b * col_part
                for axis in range(3):
                    acc[c + REACH, axis] = acc[c + REACH, axis] - row[axis]

        by_size(flag_ref, slots, body)

    return pl.pallas_call(
        kernel,
        out_shape=[
            jax.ShapeDtypeStruct((frame + 1, 3, 8, block), f32),
            jax.ShapeDtypeStruct((slots, rows, probes, block), f32),
        ],
        in_specs=[SM, SM, SM] + [VM] * 6,
        out_specs=[VM] * 2,
        scratch_shapes=[pltpu.VMEM((frame + 1, probes, block), bf16)],
        name="near_forces",
        **params(6 * slots * rows * probes * block * block, k.size * 4),
    )(flag, ids, bond, v, v_even, v_crossed, w, k, kt)


def far_forces(flag, ids, bond, v, w, w_even, w_crossed, kt, image, started):
    slots, rows, block, _ = kt.shape
    probes = v.shape[1]
    frame = rows + 2 * REACH

    def kernel(flag_ref, ids_ref, bond_ref, *refs):
        v_ref, w_ref, we_ref, wo_ref, kt_ref, image_ref, start_ref = refs[:7]
        own_ref, even_ref, odd_ref, wf, acc = refs[7:]
        odd = flag_ref[1]
        fill_frame(wf, odd, w_ref, we_ref, wo_ref)
        acc[...] = start_ref[...]

        def body(count):
            for c in range(rows):
                mine = v_ref[c].astype(f32)
                row = [jnp.zeros((8, block), f32)] * 3
                for m in range(0, count, 2):
                    two = (m, m + 1)
                    far = [wf[ids_ref[c, slot]] for slot in two]
                    weights = jnp.concatenate([kt_ref[slot, c] for slot in two], axis=1)
                    back = dot(jnp.concatenate(far, axis=0), weights, NN)
                    for i, slot in enumerate(two):
                        d = ids_ref[c, slot]
                        lanes = slice(i * block, (i + 1) * block)
                        col_part = folded(far[i].astype(f32) * image_ref[slot, c])
                        row_part = folded(mine * back[i * probes : (i + 1) * probes, lanes])
                        for axis in range(3):
                            b = bond_ref[axis * rows + c, slot]
                            row[axis] = row[axis] + b * row_part
                            acc[d, axis] = acc[d, axis] + b * col_part
                for axis in range(3):
                    acc[c + REACH, axis] = acc[c + REACH, axis] - row[axis]

        by_size(flag_ref, slots, body)

        def taken(start, count):
            return DECAY * jnp.sum(acc[pl.ds(start, count)], axis=2)

        own_ref[...] = taken(REACH, rows)
        even_ref[...] = taken((1 - odd) * (REACH + rows), REACH)
        odd_ref[...] = taken(odd * (REACH + rows), REACH)

    side = jax.ShapeDtypeStruct((REACH, 3, block), f32)
    return pl.pallas_call(
        kernel,
        out_shape=[jax.ShapeDtypeStruct((rows, 3, block), f32), side, side],
        in_specs=[SM, SM, SM] + [VM] * 7,
        out_specs=[VM] * 3,
        scratch_shapes=[
            pltpu.VMEM((frame + 1, probes, block), bf16),
            pltpu.VMEM((frame + 1, 3, 8, block), f32),
        ],
        name="far_forces",
        **params(2 * slots * rows * probes * block * block, kt.size * 2 + image.size * 4),
    )(flag, ids, bond, v, w, w_even, w_crossed, kt, image, started)


def local(probes, onsite, hopping, block_col, atom_of, bond_dir, chemical_potential):
    rows, _, block = probes.shape
    orbitals = float(rows * lax.axis_size("clus") * block)
    x = probes
    even, crossed = exchange(x, x)
    v_even, v_crossed = even, crossed
    flag, ids, at, bond, coeffs, own, to_even, to_odd, k, kt = opening(
        block_col.T, x, hopping, jnp.transpose(bond_dir, (0, 2, 1)), chemical_potential
    )
    rounds = (lax.axis_size("clus") - 1).bit_length()
    cheb = [probes]
    for term in range(1, ORDER + 1):
        if term == 3:
            sums = doubled(0, moments(coeffs, *cheb), "clus")
        if term > 1:
            to_odd = ahead(flag, at, x, k)
            own, to_even = spread(flag, ids, x, k)
        back_even, back_crossed = exchange(to_even, to_odd)
        if term > 2:
            sums = doubled(term - 2, sums, "clus")
        image = direct(flag, ids, x, even, crossed, kt, own, onsite)
        if term == ORDER:
            break
        image = image + (back_even.astype(f32) + back_crossed.astype(f32))
        cheb.append(image if term == 1 else 2.0 * image - cheb[-2].astype(f32))
        x = cheb[-1].astype(bf16)
        even, crossed = exchange(x, x)
    for index in range(3, rounds):
        sums = doubled(index, sums, "clus")
    weighted, head = closed(coeffs, sums, orbitals, cheb, image, back_even, back_crossed)
    w_even, w_crossed = exchange(weighted, weighted)
    started, image = near_forces(flag, ids, bond, probes, v_even, v_crossed, weighted, k, kt)
    own, to_even, to_odd = far_forces(
        flag, ids, bond, probes, weighted, w_even, w_crossed, kt, image, started
    )
    from_even, from_odd = exchange(to_even, to_odd)
    part = packed(head, own, from_even, from_odd, atom_of)
    count = lax.axis_size("probe")
    parts = [part]
    step = 1
    while step < count:
        part = sum(parts[1:], parts[0])
        parts = [part, lax.ppermute(part, "probe", [(i, i ^ step) for i in range(count)])]
        step *= 2
    return tuple(unpacked(parts, rows, orbitals))


def solution(mesh):
    placed = (
        P("clus", "probe", None),
        P("clus", None),
        P(None, "clus", None, None),
        P(None, "clus"),
        P("clus", None),
        P(None, None, "clus"),
        P(),
    )
    return jax.shard_map(
        local,
        mesh=mesh,
        in_specs=placed,
        out_specs=(P("clus", None), P(), P(None, "clus")),
        check_vma=False,
    )
```

```python
import functools

import jax
import jax.numpy as jnp
import numpy as np
from jax import lax
from jax.experimental import pallas as pl
from jax.experimental.pallas import tpu as pltpu
from jax.sharding import PartitionSpec as P


ATOMS = 32
REACH = 12
PROBE_VECTORS = 128
ORDER = 4
DECAY = 50.0
SMEARING_TEMP = 0.1
QUAD_NODES = 64
HALF_SLOTS = 10
CHUNKS = 3
AHEAD = 6

bf16 = jnp.bfloat16
f32 = jnp.float32
NN = (((1,), (0,)), ((), ()))
NT = (((1,), (1,)), ((), ()))
dot = functools.partial(lax.dot_general, preferred_element_type=f32)
VM = pl.BlockSpec(memory_space=pltpu.VMEM)
SM = pl.BlockSpec(memory_space=pltpu.SMEM)


def params(flops, nbytes):
    return dict(
        compiler_params=pltpu.CompilerParams(vmem_limit_bytes=8 << 20),
        cost_estimate=pl.CostEstimate(flops=flops, bytes_accessed=nbytes, transcendentals=0),
    )


def quadrature():
    angles = np.pi * (np.arange(QUAD_NODES) + 0.5) / QUAD_NODES
    table = np.zeros((8, 128), np.float32)
    for order in range(ORDER + 1):
        weight = 2.0 / QUAD_NODES * (0.5 if order == 0 else 1.0)
        table[order, :QUAD_NODES] = weight * np.cos(order * angles)
    table[7, :QUAD_NODES] = np.cos(angles)
    return jnp.asarray(table)


def opening(columns, x, k, bond_dir, chemical_potential):
    rows, slots = columns.shape
    probes, block = x.shape[1:]
    frame = rows + 2 * REACH
    halves = (0, HALF_SLOTS, slots)
    height = rows // CHUNKS

    def kernel(col_hbm, x_hbm, k_hbm, bond_hbm, table_hbm, mu_ref, *refs):
        flag_ref, ids_ref, at_ref, out_ref, coeff_ref, own_ref, even_ref, odd_ref, kv_ref, kt_ref, image_ref = refs[:11]
        acc, col_sm, col_vm, xv, bond_vm, table_vm, ids_vm, at_vm, out_vm, sems, small = refs[11:]
        me = lax.axis_index("clus")

        def load(index):
            half, chunk = divmod(index, CHUNKS)
            part = pl.ds(halves[half], halves[half + 1] - halves[half])
            group = pl.ds(chunk * height, height)
            return pltpu.make_async_copy(
                k_hbm.at[part, group], kv_ref.at[part, group], sems.at[index]
            )

        pairs = (
            (col_hbm, col_vm),
            (col_hbm, col_sm),
            (x_hbm, xv),
            (table_hbm, table_vm),
            (bond_hbm, bond_vm),
        )
        copies = [pltpu.make_async_copy(a, b, small.at[i]) for i, (a, b) in enumerate(pairs)]
        for copy in copies:
            copy.start()
        for index in range(min(AHEAD, CHUNKS)):
            load(index).start()
        acc[...] = jnp.zeros_like(acc)
        copies[0].wait()
        col = col_vm[...]
        late = lax.broadcasted_iota(jnp.int32, col.shape, 1) >= HALF_SLOTS
        many = jnp.max(jnp.where(late, col, -1)) >= 0
        flag_ref[0] = many.astype(jnp.int32)
        odd = lax.rem(me, 2)
        flag_ref[1] = odd

        ids = jnp.where(col >= 0, col - me * rows + REACH, frame)
        ids_vm[...] = ids
        side = lax.broadcasted_iota(jnp.int32, (rows, REACH), 1) + odd * (REACH + rows)
        at = jnp.full((rows, REACH), slots, jnp.int32)
        for m in range(slots):
            at = jnp.where(ids[:, m : m + 1] == side, m, at)
        at_vm[...] = at
        for c in range(rows):
            kv_ref[slots, c] = jnp.zeros((block, block), kv_ref.dtype)
            image_ref[slots, c] = jnp.zeros((probes, block), f32)
        for copy in copies[1:]:
            copy.wait()
        for axis in range(3):
            lines = slice(axis * rows, (axis + 1) * rows)
            out_vm[lines, :slots] = bond_vm[axis].astype(f32)
            out_vm[lines, slots:] = jnp.zeros((rows, 1), f32)
        tables = ((ids_vm, ids_ref), (at_vm, at_ref), (out_vm, out_ref))
        placed = [pltpu.make_async_copy(a, b, small.at[5 + i]) for i, (a, b) in enumerate(tables)]
        for copy in placed:
            copy.start()
        energy = (table_vm[7:8] - mu_ref[0]) / SMEARING_TEMP
        occupied = 1.0 / (1.0 + jnp.exp(energy))
        total = jnp.sum(table_vm[...] * occupied, axis=1, keepdims=True)
        coeff_ref[...] = jnp.broadcast_to(total, coeff_ref.shape)

        def body(last):
            for index in range(last * CHUNKS):
                half, chunk = divmod(index, CHUNKS)
                if index == 0:
                    for later in range(min(AHEAD, CHUNKS), min(AHEAD, last * CHUNKS)):
                        load(later).start()
                load(index).wait()
                if index + AHEAD < last * CHUNKS:
                    load(index + AHEAD).start()
                for c in range(chunk * height, (chunk + 1) * height):
                    xc = xv[c]
                    for first in range(halves[half], halves[half + 1], 4):
                        parts, targets = [], []
                        for m in range(first, min(first + 4, halves[half + 1]), 2):
                            pair = [kv_ref[m, c], kv_ref[m + 1, c]]
                            out = dot(xc, jnp.concatenate(pair, axis=1), NN)
                            parts += [out[:, :block], out[:, block:]]
                            for slot in (m, m + 1):
                                at = col_sm[c, slot]
                                targets.append(jnp.where(at >= 0, at - me * rows + REACH, frame))
                            image_ref[m, c] = parts[-2]
                            image_ref[m + 1, c] = parts[-1]
                            kt_ref[m, c] = pair[0].T
                            kt_ref[m + 1, c] = pair[1].T
                        values = [acc[t] + part for t, part in zip(targets, parts)]
                        for t, value in zip(targets, values):
                            acc[t] = value

        @pl.when(many)
        def _():
            body(2)

        @pl.when(jnp.logical_not(many))
        def _():
            body(1)

        own_ref[...] = acc[pl.ds(REACH, rows)]
        even_ref[...] = acc[pl.ds((1 - odd) * (REACH + rows), REACH)].astype(bf16)
        odd_ref[...] = acc[pl.ds(odd * (REACH + rows), REACH)].astype(bf16)
        for copy in placed:
            copy.wait()

    side = jax.ShapeDtypeStruct((REACH, probes, block), bf16)
    hbm = pl.BlockSpec(memory_space=pltpu.HBM)
    operands = (columns, x, k, bond_dir, quadrature())
    return pl.pallas_call(
        kernel,
        out_shape=[
            pltpu.SMEM((2,), jnp.int32),
            pltpu.SMEM((rows, slots), jnp.int32),
            pltpu.SMEM((rows, REACH), jnp.int32),
            pltpu.SMEM((3 * rows, slots + 1), f32),
            jax.ShapeDtypeStruct((8, 128), f32),
            jax.ShapeDtypeStruct((rows, probes, block), f32),
            side,
            side,
            jax.ShapeDtypeStruct((slots + 1, *k.shape[1:]), k.dtype),
            jax.ShapeDtypeStruct(k.shape, k.dtype),
            jax.ShapeDtypeStruct((slots + 1, rows, probes, block), f32),
        ],
        in_specs=[hbm] * 5 + [SM],
        out_specs=[SM] * 4 + [VM] * 7,
        scratch_shapes=[
            pltpu.VMEM((frame + 1, probes, block), f32),
            pltpu.SMEM((rows, slots), jnp.int32),
            pltpu.VMEM((rows, slots), jnp.int32),
            pltpu.VMEM(x.shape, x.dtype),
            pltpu.VMEM(bond_dir.shape, bond_dir.dtype),
            pltpu.VMEM((8, 128), f32),
            pltpu.VMEM((rows, slots), jnp.int32),
            pltpu.VMEM((rows, REACH), jnp.int32),
            pltpu.VMEM((3 * rows, slots + 1), f32),
            pltpu.SemaphoreType.DMA((2 * CHUNKS,)),
            pltpu.SemaphoreType.DMA((8,)),
        ],
        name="opening",
        **params(2 * slots * rows * probes * block * block, k.size * 2),
    )(*(pltpu.with_memory_space_constraint(a, pltpu.HBM) for a in operands), chemical_potential)


def moments(coeffs, v, first, second):
    _, probes, block = v.shape

    def kernel(coeff_ref, v_ref, a_ref, b_ref, out_ref):
        wide = v_ref[...].astype(f32)
        a, b = a_ref[...], b_ref[...]
        pairs = (wide * wide, wide * a, wide * b, a * b, b * b)
        m0, m1, m2, ab, bb = [jnp.sum(pair, axis=0) for pair in pairs]
        c = [coeff_ref[k : k + 1] for k in range(ORDER + 1)]
        out_ref[0] = m0
        out_ref[1] = (
            c[0] * m0 + c[1] * m1 + c[2] * m2 + c[3] * (2.0 * ab - m1) + c[4] * (2.0 * bb - m0)
        )

    return pl.pallas_call(
        kernel,
        out_shape=jax.ShapeDtypeStruct((2, probes, block), f32),
        in_specs=[VM] * 4,
        out_specs=VM,
        name="moments",
        **params(10 * v.size, 10 * v.size),
    )(coeffs, v, first, second)


def closed(coeffs, sums, orbitals, cheb, image, back_even, back_crossed):
    rows, probes, block = image.shape

    def kernel(coeff_ref, sum_ref, c0, c1, c2, c3, y_ref, e_ref, o_ref, w_ref, head_ref):
        square = jnp.sum(sum_ref[0], axis=1, keepdims=True)
        scale = orbitals / (square * PROBE_VECTORS)
        head_ref[...] = jnp.zeros_like(head_ref)
        head_ref[rows : rows + 1] = jnp.sum(scale * sum_ref[1], axis=0, keepdims=True)
        scale = jnp.broadcast_to(scale, (probes, block))
        c = [coeff_ref[k : k + 1] for k in range(ORDER + 1)]
        for r in range(rows):
            y = y_ref[r] + (e_ref[r].astype(f32) + o_ref[r].astype(f32))
            wide = c0[r].astype(f32)
            fermi = c[0] * wide + c[1] * c1[r]
            fermi = fermi + c[2] * c2[r]
            fermi = fermi + c[3] * c3[r]
            fermi = fermi + c[4] * (2.0 * y - c2[r])
            scaled = fermi * scale
            w_ref[r] = scaled.astype(bf16)
            head_ref[r : r + 1] = jnp.sum(wide * scaled, axis=0, keepdims=True)

    return pl.pallas_call(
        kernel,
        out_shape=[
            jax.ShapeDtypeStruct((rows, probes, block), bf16),
            jax.ShapeDtypeStruct((16, block), f32),
        ],
        in_specs=[VM] * 9,
        out_specs=[VM] * 2,
        name="closed",
        **params(20 * image.size, 30 * image.size),
    )(coeffs, sums, *cheb, image, back_even, back_crossed)


def packed(head, own, from_even, from_odd, atom_of):
    rows, _, block = own.shape
    group = block // ATOMS
    lines = rows // group

    def kernel(head_ref, own_ref, e_ref, o_ref, atom_ref, out_ref):
        out_ref[...] = jnp.zeros_like(out_ref)
        out_ref[: rows + 1] = head_ref[: rows + 1]
        lane = lax.broadcasted_iota(jnp.int32, (block, block), 0)
        for line in range(lines):
            total = jnp.zeros((16, block), f32)
            for part in range(group):
                r = line * group + part
                g = own_ref[r] + e_ref[r] + o_ref[r]
                high = g.astype(bf16)
                rest = g - high.astype(f32)
                middle = rest.astype(bf16)
                low = (rest - middle.astype(f32)).astype(bf16)
                pad = jnp.zeros((16 - 9, block), bf16)
                left = jnp.concatenate([high, middle, low, pad], axis=0)
                hot = (lane == atom_ref[r : r + 1] + part * ATOMS).astype(f32).astype(bf16)
                total = total + dot(left, hot, NT)
            value = total[0:3] + (total[3:6] + total[6:9])
            for axis in range(3):
                at = rows + 1 + axis * lines + line
                out_ref[at : at + 1] = value[axis : axis + 1]

    height = -(-(rows + 1 + 3 * lines) // 8) * 8
    return pl.pallas_call(
        kernel,
        out_shape=jax.ShapeDtypeStruct((height, block), f32),
        in_specs=[VM] * 5,
        out_specs=VM,
        name="packed",
        **params(2 * rows * 16 * block * block, 100000),
    )(head, own, from_even, from_odd, atom_of)


def unpacked(parts, rows, orbitals):
    _, block = parts[0].shape
    lines = rows * ATOMS // block

    def kernel(*refs):
        ins, (density_ref, filling_ref, force_ref) = refs[: len(parts)], refs[len(parts) :]
        total = ins[0][...]
        for other in ins[1:]:
            total = total + other[...]
        density_ref[...] = total[:rows]
        filling_ref[0] = jnp.sum(total[rows : rows + 1]) / orbitals
        for axis in range(3):
            for line in range(lines):
                at = rows + 1 + axis * lines + line
                force_ref[axis : axis + 1, line * block : (line + 1) * block] = total[at : at + 1]

    return pl.pallas_call(
        kernel,
        out_shape=[
            jax.ShapeDtypeStruct((rows, block), f32),
            jax.ShapeDtypeStruct((1,), f32),
            jax.ShapeDtypeStruct((3, lines * block), f32),
        ],
        in_specs=[VM] * len(parts),
        out_specs=[VM, SM, VM],
        name="unpacked",
        **params(10000, 100000),
    )(*parts)


def exchange(even_side, odd_side):
    count = lax.axis_size("clus")
    paired = [(i, i ^ 1) for i in range(count)]
    shifted = [(i, (i + 1 if i % 2 else i - 1) % count) for i in range(count)]
    crossed = lax.ppermute(odd_side, "clus", shifted)
    even = lax.ppermute(even_side, "clus", paired)
    return even, crossed


def doubled(index, part, axis):
    count = lax.axis_size(axis)
    other = lax.ppermute(part, axis, [(i, i ^ (1 << index)) for i in range(count)])
    return part + other


def by_size(flag, slots, body):
    @pl.when(flag[0] != 0)
    def _():
        body(slots)

    @pl.when(flag[0] == 0)
    def _():
        body(HALF_SLOTS)


def ahead(flag, at, x, k):
    _, rows, block, _ = k.shape
    probes = x.shape[1]

    def kernel(flag_ref, at_ref, x_ref, k_ref, out_ref):
        def body(above):
            for j in range(REACH):
                reach = list(range(j, rows)) if above else list(range(min(j + 1, rows)))
                acc = None
                for first in range(0, len(reach), 2):
                    group = reach[first : first + 2]
                    left = jnp.concatenate([x_ref[c] for c in group], axis=1)
                    right = jnp.concatenate([k_ref[at_ref[c, j], c] for c in group], axis=0)
                    part = dot(left, right, NN)
                    acc = part if acc is None else acc + part
                out_ref[j] = acc.astype(bf16)

        @pl.when(flag_ref[1] == 0)
        def _():
            body(False)

        @pl.when(flag_ref[1] != 0)
        def _():
            body(True)

    return pl.pallas_call(
        kernel,
        out_shape=jax.ShapeDtypeStruct((REACH, probes, block), bf16),
        in_specs=[SM, SM, VM, VM],
        out_specs=VM,
        name="ahead",
        **params(80 * 2 * probes * block * block, 80 * 2 * block * block),
    )(flag, at, x, k)


def spread(flag, ids, x, k):
    rows, slots = ids.shape
    _, probes, block = x.shape
    frame = rows + 2 * REACH

    def kernel(flag_ref, ids_ref, x_ref, k_ref, own_ref, even_ref, acc):
        acc[...] = jnp.zeros_like(acc)

        def body(count):
            for c in range(rows):
                xc = x_ref[c]
                for first in range(0, count, 4):
                    parts, targets = [], []
                    for m in range(first, min(first + 4, count), 2):
                        pair = [k_ref[m, c], k_ref[m + 1, c]]
                        out = dot(xc, jnp.concatenate(pair, axis=1), NN)
                        parts += [out[:, :block], out[:, block:]]
                        targets += [ids_ref[c, m], ids_ref[c, m + 1]]
                    values = [acc[t] + part for t, part in zip(targets, parts)]
                    for t, value in zip(targets, values):
                        acc[t] = value

        by_size(flag_ref, slots, body)
        odd = flag_ref[1]
        own_ref[...] = acc[pl.ds(REACH, rows)]
        even_ref[...] = acc[pl.ds((1 - odd) * (REACH + rows), REACH)].astype(bf16)

    side = jax.ShapeDtypeStruct((REACH, probes, block), bf16)
    return pl.pallas_call(
        kernel,
        out_shape=[jax.ShapeDtypeStruct((rows, probes, block), f32), side],
        in_specs=[SM, SM, VM, VM],
        out_specs=[VM] * 2,
        scratch_shapes=[pltpu.VMEM((frame + 1, probes, block), f32)],
        name="spread",
        **params(2 * slots * rows * probes * block * block, k.size * 2),
    )(flag, ids, x, k)


def fill_frame(frame_ref, odd, own, even, crossed):
    rows = own.shape[0]
    frame_ref[pl.ds(REACH, rows)] = own[...]
    frame_ref[pl.ds((1 - odd) * (REACH + rows), REACH)] = even[...]
    frame_ref[pl.ds(odd * (REACH + rows), REACH)] = crossed[...]
    frame_ref[rows + 2 * REACH] = jnp.zeros(own.shape[1:], own.dtype)


def direct(flag, ids, x, even, crossed, kt, own, onsite):
    slots, rows, block, _ = kt.shape
    probes = x.shape[1]

    def kernel(flag_ref, ids_ref, x_ref, e_ref, o_ref, kt_ref, own_ref, site_ref, out_ref, frame):
        fill_frame(frame, flag_ref[1], x_ref, e_ref, o_ref)

        def body(count):
            for c in range(rows):
                acc = own_ref[c] + site_ref[pl.ds(c, 1)] * x_ref[c].astype(f32)
                for m in range(0, count, 2):
                    pair = [frame[ids_ref[c, m]], frame[ids_ref[c, m + 1]]]
                    weights = jnp.concatenate([kt_ref[m, c], kt_ref[m + 1, c]], axis=0)
                    acc = acc + dot(jnp.concatenate(pair, axis=1), weights, NN)
                out_ref[c] = acc

        by_size(flag_ref, slots, body)

    return pl.pallas_call(
        kernel,
        out_shape=jax.ShapeDtypeStruct((rows, probes, block), f32),
        in_specs=[SM, SM, VM, VM, VM, VM, VM, VM],
        out_specs=VM,
        scratch_shapes=[pltpu.VMEM((rows + 2 * REACH + 1, probes, block), bf16)],
        name="direct",
        **params(2 * slots * rows * probes * block * block, kt.size * 2),
    )(flag, ids, x, even, crossed, kt, own, onsite)


def folded(value):
    parts = [value[i : i + 8] for i in range(0, value.shape[0], 8)]
    while len(parts) > 1:
        parts = [a + b for a, b in zip(parts[::2], parts[1::2])]
    return parts[0]


def turned_images(flag, ids, v, v_even, v_crossed, kt):
    slots, rows, block, _ = kt.shape
    probes = v.shape[1]

    def kernel(flag_ref, ids_ref, v_ref, ve_ref, vo_ref, kt_ref, out_ref, vf):
        fill_frame(vf, flag_ref[1], v_ref, ve_ref, vo_ref)

        def body(count):
            for c in range(rows):
                for m in range(0, count, 2):
                    two = (m, m + 1)
                    left = jnp.concatenate([vf[ids_ref[c, slot]] for slot in two], axis=0)
                    weights = jnp.concatenate([kt_ref[slot, c] for slot in two], axis=1)
                    back = dot(left, weights, NN)
                    out_ref[m, c] = back[:probes, :block]
                    out_ref[m + 1, c] = back[probes:, block:]

        by_size(flag_ref, slots, body)

    return pl.pallas_call(
        kernel,
        out_shape=jax.ShapeDtypeStruct((slots, rows, probes, block), f32),
        in_specs=[SM, SM] + [VM] * 4,
        out_specs=VM,
        scratch_shapes=[pltpu.VMEM((rows + 2 * REACH + 1, probes, block), bf16)],
        name="turned_images",
        **params(2 * slots * rows * probes * block * block, kt.size * 2),
    )(flag, ids, v, v_even, v_crossed, kt)


def near_forces(flag, ids, bond, v, v_even, v_crossed, w, k, turned):
    slots, rows, probes, block = turned.shape
    frame = rows + 2 * REACH

    def kernel(flag_ref, ids_ref, bond_ref, *refs):
        v_ref, ve_ref, vo_ref, w_ref, k_ref, turned_ref, acc, vf = refs
        fill_frame(vf, flag_ref[1], v_ref, ve_ref, vo_ref)
        acc[...] = jnp.zeros_like(acc)

        def body(count):
            for c in range(rows):
                mine = w_ref[c].astype(f32)
                row = [jnp.zeros((8, block), f32)] * 3
                for m in range(0, count, 2):
                    two = (m, m + 1)
                    weights = jnp.concatenate([k_ref[slot, c] for slot in two], axis=1)
                    out = dot(w_ref[c], weights, NN)
                    for i, slot in enumerate(two):
                        d = ids_ref[c, slot]
                        image = out[:, i * block : (i + 1) * block]
                        col_part = folded(vf[d].astype(f32) * image)
                        row_part = folded(mine * turned_ref[slot, c])
                        for axis in range(3):
                            b = bond_ref[axis * rows + c, slot]
                            row[axis] = row[axis] + b * row_part
                            acc[d, axis] = acc[d, axis] + b * col_part
                for axis in range(3):
                    acc[c + REACH, axis] = acc[c + REACH, axis] - row[axis]

        by_size(flag_ref, slots, body)

    return pl.pallas_call(
        kernel,
        out_shape=jax.ShapeDtypeStruct((frame + 1, 3, 8, block), f32),
        in_specs=[SM, SM, SM] + [VM] * 6,
        out_specs=VM,
        scratch_shapes=[pltpu.VMEM((frame + 1, probes, block), bf16)],
        name="near_forces",
        **params(2 * slots * rows * probes * block * block, k.size * 4),
    )(flag, ids, bond, v, v_even, v_crossed, w, k, turned)


def ahead_forces(flag, at, bond, w_crossed, image, started):
    rows = at.shape[0]
    block = image.shape[3]

    def kernel(flag_ref, at_ref, bond_ref, w_ref, image_ref, start_ref, out_ref):
        def body(above):
            base = REACH + rows if above else 0
            for j in range(REACH):
                theirs = w_ref[j].astype(f32)
                total = [start_ref[base + j, axis] for axis in range(3)]
                for c in range(j, rows) if above else range(min(j + 1, rows)):
                    slot = at_ref[c, j]
                    part = folded(theirs * image_ref[slot, c])
                    for axis in range(3):
                        total[axis] = total[axis] + bond_ref[axis * rows + c, slot] * part
                for axis in range(3):
                    out_ref[j, axis : axis + 1] = DECAY * jnp.sum(total[axis], axis=0, keepdims=True)

        @pl.when(flag_ref[1] == 0)
        def _():
            body(False)

        @pl.when(flag_ref[1] != 0)
        def _():
            body(True)

    return pl.pallas_call(
        kernel,
        out_shape=jax.ShapeDtypeStruct((REACH, 3, block), f32),
        in_specs=[SM, SM, SM] + [VM] * 3,
        out_specs=VM,
        name="ahead_forces",
        **params(1000000, 2000000),
    )(flag, at, bond, w_crossed, image, started)


def far_forces(flag, ids, bond, v, w, w_even, w_crossed, kt, image, started):
    slots, rows, block, _ = kt.shape
    probes = v.shape[1]
    frame = rows + 2 * REACH

    def kernel(flag_ref, ids_ref, bond_ref, *refs):
        v_ref, w_ref, we_ref, wo_ref, kt_ref, image_ref, start_ref = refs[:7]
        own_ref, even_ref, wf, acc = refs[7:]
        odd = flag_ref[1]
        fill_frame(wf, odd, w_ref, we_ref, wo_ref)
        acc[...] = start_ref[...]

        def body(count):
            for c in range(rows):
                mine = v_ref[c].astype(f32)
                row = [jnp.zeros((8, block), f32)] * 3
                for m in range(0, count, 2):
                    two = (m, m + 1)
                    far = [wf[ids_ref[c, slot]] for slot in two]
                    weights = jnp.concatenate([kt_ref[slot, c] for slot in two], axis=1)
                    back = dot(jnp.concatenate(far, axis=0), weights, NN)
                    for i, slot in enumerate(two):
                        d = ids_ref[c, slot]
                        lanes = slice(i * block, (i + 1) * block)
                        col_part = folded(far[i].astype(f32) * image_ref[slot, c])
                        row_part = folded(mine * back[i * probes : (i + 1) * probes, lanes])
                        for axis in range(3):
                            b = bond_ref[axis * rows + c, slot]
                            row[axis] = row[axis] + b * row_part
                            acc[d, axis] = acc[d, axis] + b * col_part
                for axis in range(3):
                    acc[c + REACH, axis] = acc[c + REACH, axis] - row[axis]

        by_size(flag_ref, slots, body)

        def taken(start, count):
            return DECAY * jnp.sum(acc[pl.ds(start, count)], axis=2)

        own_ref[...] = taken(REACH, rows)
        even_ref[...] = taken((1 - odd) * (REACH + rows), REACH)

    return pl.pallas_call(
        kernel,
        out_shape=[
            jax.ShapeDtypeStruct((rows, 3, block), f32),
            jax.ShapeDtypeStruct((REACH, 3, block), f32),
        ],
        in_specs=[SM, SM, SM] + [VM] * 7,
        out_specs=[VM] * 2,
        scratch_shapes=[
            pltpu.VMEM((frame + 1, probes, block), bf16),
            pltpu.VMEM((frame + 1, 3, 8, block), f32),
        ],
        name="far_forces",
        **params(2 * slots * rows * probes * block * block, kt.size * 2 + image.size * 4),
    )(flag, ids, bond, v, w, w_even, w_crossed, kt, image, started)


def local(probes, onsite, hopping, block_col, atom_of, bond_dir, chemical_potential):
    rows, _, block = probes.shape
    orbitals = float(rows * lax.axis_size("clus") * block)
    x = probes
    even, crossed = exchange(x, x)
    v_even, v_crossed = even, crossed
    flag, ids, at, bond, coeffs, own, to_even, to_odd, k, kt, kept = opening(
        block_col.T, x, hopping, jnp.transpose(bond_dir, (0, 2, 1)), chemical_potential
    )
    flag, ids, at, bond = (
        pltpu.with_memory_space_constraint(a, pltpu.SMEM) for a in (flag, ids, at, bond)
    )
    rounds = (lax.axis_size("clus") - 1).bit_length()
    cheb = [probes]
    for term in range(1, ORDER + 1):
        if term == 3:
            sums = doubled(0, moments(coeffs, *cheb), "clus")
        if term > 1:
            to_odd = ahead(flag, at, x, k)
            own, to_even = spread(flag, ids, x, k)
        back_even, back_crossed = exchange(to_even, to_odd)
        if term > 2:
            sums = doubled(term - 2, sums, "clus")
        if term == 1:
            turned = turned_images(flag, ids, x, even, crossed, kt)
        image = direct(flag, ids, x, even, crossed, kt, own, onsite)
        if term == ORDER:
            break
        image = image + (back_even.astype(f32) + back_crossed.astype(f32))
        cheb.append(image if term == 1 else 2.0 * image - cheb[-2].astype(f32))
        x = cheb[-1].astype(bf16)
        even, crossed = exchange(x, x)
    for index in range(3, rounds):
        sums = doubled(index, sums, "clus")
    weighted, head = closed(coeffs, sums, orbitals, cheb, image, back_even, back_crossed)
    w_even, w_crossed = exchange(weighted, weighted)
    started = near_forces(flag, ids, bond, probes, v_even, v_crossed, weighted, k, turned)
    to_odd = ahead_forces(flag, at, bond, w_crossed, kept, started)
    own, to_even = far_forces(
        flag, ids, bond, probes, weighted, w_even, w_crossed, kt, kept, started
    )
    from_even, from_odd = exchange(to_even, to_odd)
    part = packed(head, own, from_even, from_odd, atom_of)
    count = lax.axis_size("probe")
    parts = [part]
    step = 1
    while step < count:
        part = sum(parts[1:], parts[0])
        parts = [part, lax.ppermute(part, "probe", [(i, i ^ step) for i in range(count)])]
        step *= 2
    return tuple(unpacked(parts, rows, orbitals))


def solution(mesh):
    placed = (
        P("clus", "probe", None),
        P("clus", None),
        P(None, "clus", None, None),
        P(None, "clus"),
        P("clus", None),
        P(None, None, "clus"),
        P(),
    )
    return jax.shard_map(
        local,
        mesh=mesh,
        in_specs=placed,
        out_specs=(P("clus", None), P(), P(None, "clus")),
        check_vma=False,
    )
```

```python
import functools

import jax
import jax.numpy as jnp
import numpy as np
from jax import lax
from jax.experimental import pallas as pl
from jax.experimental.pallas import tpu as pltpu
from jax.sharding import PartitionSpec as P


ATOMS = 32
REACH = 12
PROBE_VECTORS = 128
ORDER = 4
DECAY = 50.0
SMEARING_TEMP = 0.1
QUAD_NODES = 64
HALF_SLOTS = 10
CHUNKS = 3
AHEAD = 6

bf16 = jnp.bfloat16
f32 = jnp.float32
NN = (((1,), (0,)), ((), ()))
NT = (((1,), (1,)), ((), ()))
dot = functools.partial(lax.dot_general, preferred_element_type=f32)
VM = pl.BlockSpec(memory_space=pltpu.VMEM)
SM = pl.BlockSpec(memory_space=pltpu.SMEM)


def params(flops, nbytes):
    return dict(
        compiler_params=pltpu.CompilerParams(vmem_limit_bytes=8 << 20),
        cost_estimate=pl.CostEstimate(flops=flops, bytes_accessed=nbytes, transcendentals=0),
    )


def quadrature():
    angles = np.pi * (np.arange(QUAD_NODES) + 0.5) / QUAD_NODES
    table = np.zeros((8, 128), np.float32)
    for order in range(ORDER + 1):
        weight = 2.0 / QUAD_NODES * (0.5 if order == 0 else 1.0)
        table[order, :QUAD_NODES] = weight * np.cos(order * angles)
    table[7, :QUAD_NODES] = np.cos(angles)
    return jnp.asarray(table)


def opening(columns, x, k, bond_dir):
    rows, slots = columns.shape
    probes, block = x.shape[1:]
    frame = rows + 2 * REACH
    halves = (0, HALF_SLOTS, slots)
    height = rows // CHUNKS

    def kernel(col_hbm, x_hbm, k_hbm, bond_hbm, *refs):
        flag_ref, ids_ref, at_ref, out_ref, own_ref, even_ref, odd_ref, kv_ref, kt_ref, image_ref = refs[:10]
        acc, col_sm, col_vm, xv, bond_vm, ids_vm, at_vm, out_vm, sems, small = refs[10:]
        me = lax.axis_index("clus")

        def load(index):
            half, chunk = divmod(index, CHUNKS)
            part = pl.ds(halves[half], halves[half + 1] - halves[half])
            group = pl.ds(chunk * height, height)
            return pltpu.make_async_copy(
                k_hbm.at[part, group], kv_ref.at[part, group], sems.at[index]
            )

        pairs = (
            (col_hbm, col_vm),
            (col_hbm, col_sm),
            (x_hbm, xv),
            (bond_hbm, bond_vm),
        )
        copies = [pltpu.make_async_copy(a, b, small.at[i]) for i, (a, b) in enumerate(pairs)]
        for copy in copies:
            copy.start()
        for index in range(min(AHEAD, CHUNKS)):
            load(index).start()
        acc[...] = jnp.zeros_like(acc)
        copies[0].wait()
        col = col_vm[...]
        late = lax.broadcasted_iota(jnp.int32, col.shape, 1) >= HALF_SLOTS
        many = jnp.max(jnp.where(late, col, -1)) >= 0
        flag_ref[0] = many.astype(jnp.int32)
        odd = lax.rem(me, 2)
        flag_ref[1] = odd

        ids = jnp.where(col >= 0, col - me * rows + REACH, frame)
        ids_vm[...] = ids
        side = lax.broadcasted_iota(jnp.int32, (rows, REACH), 1) + odd * (REACH + rows)
        at = jnp.full((rows, REACH), slots, jnp.int32)
        for m in range(slots):
            at = jnp.where(ids[:, m : m + 1] == side, m, at)
        at_vm[...] = at
        for c in range(rows):
            kv_ref[slots, c] = jnp.zeros((block, block), kv_ref.dtype)
            image_ref[slots, c] = jnp.zeros((probes, block), f32)
        for copy in copies[1:]:
            copy.wait()
        for axis in range(3):
            lines = slice(axis * rows, (axis + 1) * rows)
            out_vm[lines, :slots] = bond_vm[axis].astype(f32)
            out_vm[lines, slots:] = jnp.zeros((rows, 1), f32)
        tables = ((ids_vm, ids_ref), (at_vm, at_ref), (out_vm, out_ref))
        placed = [pltpu.make_async_copy(a, b, small.at[4 + i]) for i, (a, b) in enumerate(tables)]
        for copy in placed:
            copy.start()

        def body(last):
            for index in range(last * CHUNKS):
                half, chunk = divmod(index, CHUNKS)
                if index == 0:
                    for later in range(min(AHEAD, CHUNKS), min(AHEAD, last * CHUNKS)):
                        load(later).start()
                load(index).wait()
                if index + AHEAD < last * CHUNKS:
                    load(index + AHEAD).start()
                for c in range(chunk * height, (chunk + 1) * height):
                    xc = xv[c]
                    for first in range(halves[half], halves[half + 1], 4):
                        parts, targets = [], []
                        for m in range(first, min(first + 4, halves[half + 1]), 2):
                            pair = [kv_ref[m, c], kv_ref[m + 1, c]]
                            out = dot(xc, jnp.concatenate(pair, axis=1), NN)
                            parts += [out[:, :block], out[:, block:]]
                            for slot in (m, m + 1):
                                at = col_sm[c, slot]
                                targets.append(jnp.where(at >= 0, at - me * rows + REACH, frame))
                            image_ref[m, c] = parts[-2]
                            image_ref[m + 1, c] = parts[-1]
                            kt_ref[m, c] = pair[0].T
                            kt_ref[m + 1, c] = pair[1].T
                        values = [acc[t] + part for t, part in zip(targets, parts)]
                        for t, value in zip(targets, values):
                            acc[t] = value

        @pl.when(many)
        def _():
            body(2)

        @pl.when(jnp.logical_not(many))
        def _():
            body(1)

        own_ref[...] = acc[pl.ds(REACH, rows)]
        even_ref[...] = acc[pl.ds((1 - odd) * (REACH + rows), REACH)].astype(bf16)
        odd_ref[...] = acc[pl.ds(odd * (REACH + rows), REACH)].astype(bf16)
        for copy in placed:
            copy.wait()

    side = jax.ShapeDtypeStruct((REACH, probes, block), bf16)
    hbm = pl.BlockSpec(memory_space=pltpu.HBM)
    operands = (columns, x, k, bond_dir)
    return pl.pallas_call(
        kernel,
        out_shape=[
            pltpu.SMEM((2,), jnp.int32),
            pltpu.SMEM((rows, slots), jnp.int32),
            pltpu.SMEM((rows, REACH), jnp.int32),
            pltpu.SMEM((3 * rows, slots + 1), f32),
            jax.ShapeDtypeStruct((rows, probes, block), f32),
            side,
            side,
            jax.ShapeDtypeStruct((slots + 1, *k.shape[1:]), k.dtype),
            jax.ShapeDtypeStruct(k.shape, k.dtype),
            jax.ShapeDtypeStruct((slots + 1, rows, probes, block), f32),
        ],
        in_specs=[hbm] * 4,
        out_specs=[SM] * 4 + [VM] * 6,
        scratch_shapes=[
            pltpu.VMEM((frame + 1, probes, block), f32),
            pltpu.SMEM((rows, slots), jnp.int32),
            pltpu.VMEM((rows, slots), jnp.int32),
            pltpu.VMEM(x.shape, x.dtype),
            pltpu.VMEM(bond_dir.shape, bond_dir.dtype),
            pltpu.VMEM((rows, slots), jnp.int32),
            pltpu.VMEM((rows, REACH), jnp.int32),
            pltpu.VMEM((3 * rows, slots + 1), f32),
            pltpu.SemaphoreType.DMA((2 * CHUNKS,)),
            pltpu.SemaphoreType.DMA((7,)),
        ],
        name="opening",
        **params(2 * slots * rows * probes * block * block, k.size * 2),
    )(*(pltpu.with_memory_space_constraint(a, pltpu.HBM) for a in operands))


def coefficients(chemical_potential):
    def kernel(table_ref, mu_ref, out_ref):
        energy = (table_ref[7:8] - mu_ref[0]) / SMEARING_TEMP
        occupied = 1.0 / (1.0 + jnp.exp(energy))
        total = jnp.sum(table_ref[...] * occupied, axis=1, keepdims=True)
        out_ref[...] = jnp.broadcast_to(total, out_ref.shape)

    return pl.pallas_call(
        kernel,
        out_shape=jax.ShapeDtypeStruct((8, 128), f32),
        in_specs=[VM, SM],
        out_specs=VM,
        name="coefficients",
        **params(10000, 8192),
    )(quadrature(), chemical_potential)


def moments(coeffs, v, first, second):
    _, probes, block = v.shape

    def kernel(coeff_ref, v_ref, a_ref, b_ref, out_ref):
        wide = v_ref[...].astype(f32)
        a, b = a_ref[...], b_ref[...]
        pairs = (wide * wide, wide * a, wide * b, a * b, b * b)
        m0, m1, m2, ab, bb = [jnp.sum(pair, axis=0) for pair in pairs]
        c = [coeff_ref[k : k + 1] for k in range(ORDER + 1)]
        out_ref[0] = m0
        out_ref[1] = (
            c[0] * m0 + c[1] * m1 + c[2] * m2 + c[3] * (2.0 * ab - m1) + c[4] * (2.0 * bb - m0)
        )

    return pl.pallas_call(
        kernel,
        out_shape=jax.ShapeDtypeStruct((2, probes, block), f32),
        in_specs=[VM] * 4,
        out_specs=VM,
        name="moments",
        **params(10 * v.size, 10 * v.size),
    )(coeffs, v, first, second)


def closed(coeffs, sums, orbitals, cheb, image, back_even, back_crossed):
    rows, probes, block = image.shape

    def kernel(coeff_ref, sum_ref, c0, c1, c2, c3, y_ref, e_ref, o_ref, w_ref, head_ref):
        square = jnp.sum(sum_ref[0], axis=1, keepdims=True)
        scale = orbitals / (square * PROBE_VECTORS)
        head_ref[...] = jnp.zeros_like(head_ref)
        head_ref[rows : rows + 1] = jnp.sum(scale * sum_ref[1], axis=0, keepdims=True)
        scale = jnp.broadcast_to(scale, (probes, block))
        c = [coeff_ref[k : k + 1] for k in range(ORDER + 1)]
        for r in range(rows):
            y = y_ref[r] + (e_ref[r].astype(f32) + o_ref[r].astype(f32))
            wide = c0[r].astype(f32)
            fermi = c[0] * wide + c[1] * c1[r]
            fermi = fermi + c[2] * c2[r]
            fermi = fermi + c[3] * c3[r]
            fermi = fermi + c[4] * (2.0 * y - c2[r])
            scaled = fermi * scale
            w_ref[r] = scaled.astype(bf16)
            head_ref[r : r + 1] = jnp.sum(wide * scaled, axis=0, keepdims=True)

    return pl.pallas_call(
        kernel,
        out_shape=[
            jax.ShapeDtypeStruct((rows, probes, block), bf16),
            jax.ShapeDtypeStruct((16, block), f32),
        ],
        in_specs=[VM] * 9,
        out_specs=[VM] * 2,
        name="closed",
        **params(20 * image.size, 30 * image.size),
    )(coeffs, sums, *cheb, image, back_even, back_crossed)


def packed(head, own, from_even, from_odd, atom_of):
    rows, _, block = own.shape
    group = block // ATOMS
    lines = rows // group

    def kernel(head_ref, own_ref, e_ref, o_ref, atom_ref, out_ref):
        out_ref[...] = jnp.zeros_like(out_ref)
        out_ref[: rows + 1] = head_ref[: rows + 1]
        lane = lax.broadcasted_iota(jnp.int32, (block, block), 0)
        for line in range(lines):
            total = jnp.zeros((16, block), f32)
            for part in range(group):
                r = line * group + part
                g = own_ref[r] + e_ref[r] + o_ref[r]
                high = g.astype(bf16)
                rest = g - high.astype(f32)
                middle = rest.astype(bf16)
                low = (rest - middle.astype(f32)).astype(bf16)
                pad = jnp.zeros((16 - 9, block), bf16)
                left = jnp.concatenate([high, middle, low, pad], axis=0)
                hot = (lane == atom_ref[r : r + 1] + part * ATOMS).astype(f32).astype(bf16)
                total = total + dot(left, hot, NT)
            value = total[0:3] + (total[3:6] + total[6:9])
            for axis in range(3):
                at = rows + 1 + axis * lines + line
                out_ref[at : at + 1] = value[axis : axis + 1]

    height = -(-(rows + 1 + 3 * lines) // 8) * 8
    return pl.pallas_call(
        kernel,
        out_shape=jax.ShapeDtypeStruct((height, block), f32),
        in_specs=[VM] * 5,
        out_specs=VM,
        name="packed",
        **params(2 * rows * 16 * block * block, 100000),
    )(head, own, from_even, from_odd, atom_of)


def unpacked(parts, rows, orbitals):
    _, block = parts[0].shape
    lines = rows * ATOMS // block

    def kernel(*refs):
        ins, (density_ref, filling_ref, force_ref) = refs[: len(parts)], refs[len(parts) :]
        total = ins[0][...]
        for other in ins[1:]:
            total = total + other[...]
        density_ref[...] = total[:rows]
        filling_ref[0] = jnp.sum(total[rows : rows + 1]) / orbitals
        for axis in range(3):
            for line in range(lines):
                at = rows + 1 + axis * lines + line
                force_ref[axis : axis + 1, line * block : (line + 1) * block] = total[at : at + 1]

    return pl.pallas_call(
        kernel,
        out_shape=[
            jax.ShapeDtypeStruct((rows, block), f32),
            jax.ShapeDtypeStruct((1,), f32),
            jax.ShapeDtypeStruct((3, lines * block), f32),
        ],
        in_specs=[VM] * len(parts),
        out_specs=[VM, SM, VM],
        name="unpacked",
        **params(10000, 100000),
    )(*parts)


def exchange(even_side, odd_side):
    count = lax.axis_size("clus")
    paired = [(i, i ^ 1) for i in range(count)]
    shifted = [(i, (i + 1 if i % 2 else i - 1) % count) for i in range(count)]
    crossed = lax.ppermute(odd_side, "clus", shifted)
    even = lax.ppermute(even_side, "clus", paired)
    return even, crossed


def doubled(index, part, axis):
    count = lax.axis_size(axis)
    other = lax.ppermute(part, axis, [(i, i ^ (1 << index)) for i in range(count)])
    return part + other


def by_size(flag, slots, body):
    @pl.when(flag[0] != 0)
    def _():
        body(slots)

    @pl.when(flag[0] == 0)
    def _():
        body(HALF_SLOTS)


def ahead(flag, at, x, k):
    _, rows, block, _ = k.shape
    probes = x.shape[1]

    def kernel(flag_ref, at_ref, x_ref, k_ref, out_ref):
        def body(above):
            for j in range(REACH):
                reach = list(range(j, rows)) if above else list(range(min(j + 1, rows)))
                acc = None
                for first in range(0, len(reach), 2):
                    group = reach[first : first + 2]
                    left = jnp.concatenate([x_ref[c] for c in group], axis=1)
                    right = jnp.concatenate([k_ref[at_ref[c, j], c] for c in group], axis=0)
                    part = dot(left, right, NN)
                    acc = part if acc is None else acc + part
                out_ref[j] = acc.astype(bf16)

        @pl.when(flag_ref[1] == 0)
        def _():
            body(False)

        @pl.when(flag_ref[1] != 0)
        def _():
            body(True)

    return pl.pallas_call(
        kernel,
        out_shape=jax.ShapeDtypeStruct((REACH, probes, block), bf16),
        in_specs=[SM, SM, VM, VM],
        out_specs=VM,
        name="ahead",
        **params(80 * 2 * probes * block * block, 80 * 2 * block * block),
    )(flag, at, x, k)


def spread(flag, ids, x, k):
    rows, slots = ids.shape
    _, probes, block = x.shape
    frame = rows + 2 * REACH

    def kernel(flag_ref, ids_ref, x_ref, k_ref, own_ref, even_ref, acc):
        acc[...] = jnp.zeros_like(acc)

        def body(count):
            for c in range(rows):
                xc = x_ref[c]
                for first in range(0, count, 4):
                    parts, targets = [], []
                    for m in range(first, min(first + 4, count), 2):
                        pair = [k_ref[m, c], k_ref[m + 1, c]]
                        out = dot(xc, jnp.concatenate(pair, axis=1), NN)
                        parts += [out[:, :block], out[:, block:]]
                        targets += [ids_ref[c, m], ids_ref[c, m + 1]]
                    values = [acc[t] + part for t, part in zip(targets, parts)]
                    for t, value in zip(targets, values):
                        acc[t] = value

        by_size(flag_ref, slots, body)
        odd = flag_ref[1]
        own_ref[...] = acc[pl.ds(REACH, rows)]
        even_ref[...] = acc[pl.ds((1 - odd) * (REACH + rows), REACH)].astype(bf16)

    side = jax.ShapeDtypeStruct((REACH, probes, block), bf16)
    return pl.pallas_call(
        kernel,
        out_shape=[jax.ShapeDtypeStruct((rows, probes, block), f32), side],
        in_specs=[SM, SM, VM, VM],
        out_specs=[VM] * 2,
        scratch_shapes=[pltpu.VMEM((frame + 1, probes, block), f32)],
        name="spread",
        **params(2 * slots * rows * probes * block * block, k.size * 2),
    )(flag, ids, x, k)


def fill_frame(frame_ref, odd, own, even, crossed):
    rows = own.shape[0]
    frame_ref[pl.ds(REACH, rows)] = own[...]
    frame_ref[pl.ds((1 - odd) * (REACH + rows), REACH)] = even[...]
    frame_ref[pl.ds(odd * (REACH + rows), REACH)] = crossed[...]
    frame_ref[rows + 2 * REACH] = jnp.zeros(own.shape[1:], own.dtype)


def direct(flag, ids, x, even, crossed, kt, own, onsite):
    slots, rows, block, _ = kt.shape
    probes = x.shape[1]

    def kernel(flag_ref, ids_ref, x_ref, e_ref, o_ref, kt_ref, own_ref, site_ref, out_ref, frame):
        fill_frame(frame, flag_ref[1], x_ref, e_ref, o_ref)

        def body(count):
            for c in range(rows):
                acc = own_ref[c] + site_ref[pl.ds(c, 1)] * x_ref[c].astype(f32)
                for m in range(0, count, 2):
                    pair = [frame[ids_ref[c, m]], frame[ids_ref[c, m + 1]]]
                    weights = jnp.concatenate([kt_ref[m, c], kt_ref[m + 1, c]], axis=0)
                    acc = acc + dot(jnp.concatenate(pair, axis=1), weights, NN)
                out_ref[c] = acc

        by_size(flag_ref, slots, body)

    return pl.pallas_call(
        kernel,
        out_shape=jax.ShapeDtypeStruct((rows, probes, block), f32),
        in_specs=[SM, SM, VM, VM, VM, VM, VM, VM],
        out_specs=VM,
        scratch_shapes=[pltpu.VMEM((rows + 2 * REACH + 1, probes, block), bf16)],
        name="direct",
        **params(2 * slots * rows * probes * block * block, kt.size * 2),
    )(flag, ids, x, even, crossed, kt, own, onsite)


def folded(value):
    parts = [value[i : i + 8] for i in range(0, value.shape[0], 8)]
    while len(parts) > 1:
        parts = [a + b for a, b in zip(parts[::2], parts[1::2])]
    return parts[0]


def turned_images(flag, ids, v, v_even, v_crossed, kt):
    slots, rows, block, _ = kt.shape
    probes = v.shape[1]

    def kernel(flag_ref, ids_ref, v_ref, ve_ref, vo_ref, kt_ref, out_ref, vf):
        fill_frame(vf, flag_ref[1], v_ref, ve_ref, vo_ref)

        def body(count):
            for c in range(rows):
                for m in range(0, count, 2):
                    two = (m, m + 1)
                    left = jnp.concatenate([vf[ids_ref[c, slot]] for slot in two], axis=0)
                    weights = jnp.concatenate([kt_ref[slot, c] for slot in two], axis=1)
                    back = dot(left, weights, NN)
                    out_ref[m, c] = back[:probes, :block]
                    out_ref[m + 1, c] = back[probes:, block:]

        by_size(flag_ref, slots, body)

    return pl.pallas_call(
        kernel,
        out_shape=jax.ShapeDtypeStruct((slots, rows, probes, block), f32),
        in_specs=[SM, SM] + [VM] * 4,
        out_specs=VM,
        scratch_shapes=[pltpu.VMEM((rows + 2 * REACH + 1, probes, block), bf16)],
        name="turned_images",
        **params(2 * slots * rows * probes * block * block, kt.size * 2),
    )(flag, ids, v, v_even, v_crossed, kt)


def near_forces(flag, ids, bond, v, v_even, v_crossed, w, k, turned):
    slots, rows, probes, block = turned.shape
    frame = rows + 2 * REACH

    def kernel(flag_ref, ids_ref, bond_ref, *refs):
        v_ref, ve_ref, vo_ref, w_ref, k_ref, turned_ref, acc, vf = refs
        fill_frame(vf, flag_ref[1], v_ref, ve_ref, vo_ref)
        acc[...] = jnp.zeros_like(acc)

        def body(count):
            for c in range(rows):
                mine = w_ref[c].astype(f32)
                row = [jnp.zeros((8, block), f32)] * 3
                for m in range(0, count, 2):
                    two = (m, m + 1)
                    weights = jnp.concatenate([k_ref[slot, c] for slot in two], axis=1)
                    out = dot(w_ref[c], weights, NN)
                    for i, slot in enumerate(two):
                        d = ids_ref[c, slot]
                        image = out[:, i * block : (i + 1) * block]
                        col_part = folded(vf[d].astype(f32) * image)
                        row_part = folded(mine * turned_ref[slot, c])
                        for axis in range(3):
                            b = bond_ref[axis * rows + c, slot]
                            row[axis] = row[axis] + b * row_part
                            acc[d, axis] = acc[d, axis] + b * col_part
                for axis in range(3):
                    acc[c + REACH, axis] = acc[c + REACH, axis] - row[axis]

        by_size(flag_ref, slots, body)

    return pl.pallas_call(
        kernel,
        out_shape=jax.ShapeDtypeStruct((frame + 1, 3, 8, block), f32),
        in_specs=[SM, SM, SM] + [VM] * 6,
        out_specs=VM,
        scratch_shapes=[pltpu.VMEM((frame + 1, probes, block), bf16)],
        name="near_forces",
        **params(2 * slots * rows * probes * block * block, k.size * 4),
    )(flag, ids, bond, v, v_even, v_crossed, w, k, turned)


def ahead_forces(flag, at, bond, w_crossed, image, started):
    rows = at.shape[0]
    block = image.shape[3]

    def kernel(flag_ref, at_ref, bond_ref, w_ref, image_ref, start_ref, out_ref):
        def body(above):
            base = REACH + rows if above else 0
            for j in range(REACH):
                theirs = w_ref[j].astype(f32)
                total = [start_ref[base + j, axis] for axis in range(3)]
                for c in range(j, rows) if above else range(min(j + 1, rows)):
                    slot = at_ref[c, j]
                    part = folded(theirs * image_ref[slot, c])
                    for axis in range(3):
                        total[axis] = total[axis] + bond_ref[axis * rows + c, slot] * part
                for axis in range(3):
                    out_ref[j, axis : axis + 1] = DECAY * jnp.sum(total[axis], axis=0, keepdims=True)

        @pl.when(flag_ref[1] == 0)
        def _():
            body(False)

        @pl.when(flag_ref[1] != 0)
        def _():
            body(True)

    return pl.pallas_call(
        kernel,
        out_shape=jax.ShapeDtypeStruct((REACH, 3, block), f32),
        in_specs=[SM, SM, SM] + [VM] * 3,
        out_specs=VM,
        name="ahead_forces",
        **params(1000000, 2000000),
    )(flag, at, bond, w_crossed, image, started)


def far_forces(flag, ids, bond, v, w, w_even, w_crossed, kt, image, started):
    slots, rows, block, _ = kt.shape
    probes = v.shape[1]
    frame = rows + 2 * REACH

    def kernel(flag_ref, ids_ref, bond_ref, *refs):
        v_ref, w_ref, we_ref, wo_ref, kt_ref, image_ref, start_ref = refs[:7]
        own_ref, even_ref, wf, acc = refs[7:]
        odd = flag_ref[1]
        fill_frame(wf, odd, w_ref, we_ref, wo_ref)
        acc[...] = start_ref[...]

        def body(count):
            for c in range(rows):
                mine = v_ref[c].astype(f32)
                row = [jnp.zeros((8, block), f32)] * 3
                for m in range(0, count, 2):
                    two = (m, m + 1)
                    far = [wf[ids_ref[c, slot]] for slot in two]
                    weights = jnp.concatenate([kt_ref[slot, c] for slot in two], axis=1)
                    back = dot(jnp.concatenate(far, axis=0), weights, NN)
                    for i, slot in enumerate(two):
                        d = ids_ref[c, slot]
                        lanes = slice(i * block, (i + 1) * block)
                        col_part = folded(far[i].astype(f32) * image_ref[slot, c])
                        row_part = folded(mine * back[i * probes : (i + 1) * probes, lanes])
                        for axis in range(3):
                            b = bond_ref[axis * rows + c, slot]
                            row[axis] = row[axis] + b * row_part
                            acc[d, axis] = acc[d, axis] + b * col_part
                for axis in range(3):
                    acc[c + REACH, axis] = acc[c + REACH, axis] - row[axis]

        by_size(flag_ref, slots, body)

        def taken(start, count):
            return DECAY * jnp.sum(acc[pl.ds(start, count)], axis=2)

        own_ref[...] = taken(REACH, rows)
        even_ref[...] = taken((1 - odd) * (REACH + rows), REACH)

    return pl.pallas_call(
        kernel,
        out_shape=[
            jax.ShapeDtypeStruct((rows, 3, block), f32),
            jax.ShapeDtypeStruct((REACH, 3, block), f32),
        ],
        in_specs=[SM, SM, SM] + [VM] * 7,
        out_specs=[VM] * 2,
        scratch_shapes=[
            pltpu.VMEM((frame + 1, probes, block), bf16),
            pltpu.VMEM((frame + 1, 3, 8, block), f32),
        ],
        name="far_forces",
        **params(2 * slots * rows * probes * block * block, kt.size * 2 + image.size * 4),
    )(flag, ids, bond, v, w, w_even, w_crossed, kt, image, started)


def local(probes, onsite, hopping, block_col, atom_of, bond_dir, chemical_potential):
    rows, _, block = probes.shape
    orbitals = float(rows * lax.axis_size("clus") * block)
    x = probes
    even, crossed = exchange(x, x)
    v_even, v_crossed = even, crossed
    flag, ids, at, bond, own, to_even, to_odd, k, kt, kept = opening(
        block_col.T, x, hopping, jnp.transpose(bond_dir, (0, 2, 1))
    )
    flag, ids, at, bond = (
        pltpu.with_memory_space_constraint(a, pltpu.SMEM) for a in (flag, ids, at, bond)
    )
    rounds = (lax.axis_size("clus") - 1).bit_length()
    cheb = [probes]
    for term in range(1, ORDER + 1):
        if term == 3:
            sums = doubled(0, moments(coeffs, *cheb), "clus")
        if term > 1:
            to_odd = ahead(flag, at, x, k)
            own, to_even = spread(flag, ids, x, k)
        back_even, back_crossed = exchange(to_even, to_odd)
        if term > 2:
            sums = doubled(term - 2, sums, "clus")
        if term == 1:
            coeffs = coefficients(chemical_potential)
            turned = turned_images(flag, ids, x, even, crossed, kt)
        image = direct(flag, ids, x, even, crossed, kt, own, onsite)
        if term == ORDER:
            break
        image = image + (back_even.astype(f32) + back_crossed.astype(f32))
        cheb.append(image if term == 1 else 2.0 * image - cheb[-2].astype(f32))
        x = cheb[-1].astype(bf16)
        even, crossed = exchange(x, x)
    for index in range(3, rounds):
        sums = doubled(index, sums, "clus")
    weighted, head = closed(coeffs, sums, orbitals, cheb, image, back_even, back_crossed)
    w_even, w_crossed = exchange(weighted, weighted)
    started = near_forces(flag, ids, bond, probes, v_even, v_crossed, weighted, k, turned)
    to_odd = ahead_forces(flag, at, bond, w_crossed, kept, started)
    own, to_even = far_forces(
        flag, ids, bond, probes, weighted, w_even, w_crossed, kt, kept, started
    )
    from_even, from_odd = exchange(to_even, to_odd)
    part = packed(head, own, from_even, from_odd, atom_of)
    count = lax.axis_size("probe")
    parts = [part]
    step = 1
    while step < count:
        part = sum(parts[1:], parts[0])
        parts = [part, lax.ppermute(part, "probe", [(i, i ^ step) for i in range(count)])]
        step *= 2
    return tuple(unpacked(parts, rows, orbitals))


def solution(mesh):
    placed = (
        P("clus", "probe", None),
        P("clus", None),
        P(None, "clus", None, None),
        P(None, "clus"),
        P("clus", None),
        P(None, None, "clus"),
        P(),
    )
    return jax.shard_map(
        local,
        mesh=mesh,
        in_specs=placed,
        out_specs=(P("clus", None), P(), P(None, "clus")),
        check_vma=False,
    )
```
